128 devices in a mesh: dp: 4 (over x_hi, core), tensor: 8 (over y, x_lo), layer: 4 (over z).
Axes of the slice: x: 4 (x_hi: 2, x_lo: 2; x = x_hi * 2 + x_lo), y: 4, z: 4, core: 2. Of those that a mesh axis runs over, the one named last changes fastest.
Arguments:
- saved_inputs: bfloat16 [4, 2048, 8192], P(None, 'dp', ('tensor', 'layer')), may hold values from -6 to 6
- output_grad: bfloat16 [2048, 8192], P('dp', ('tensor', 'layer')), may hold values from -4 to 4
- weights: bfloat16 [4, 8192, 8, 4, 256], P(None, 'tensor', None, 'layer'), may hold values from -0.0625 to 0.0625
- proj_in: bfloat16 [4, 64, 8192], P(None, None, ('tensor', 'layer')), may hold values from -0.0625 to 0.0625
- proj_out: bfloat16 [4, 64, 8192], P(None, None, ('tensor', 'layer')), may hold values from -0.0625 to 0.0625
- query_grads: bfloat16 [4, 4096, 4096], P('layer', ('dp', 'tensor')), may hold values from -0.00390625 to 0.00390625
- owner_map: int32 [4], replicated, may hold values from 0 to 3, each once
Outputs:
- input_grad: bfloat16 [2048, 8192], P('dp', ('tensor', 'layer'))
- scores: float32 [4, 4096], P('layer', ('dp', 'tensor'))
The draws below stay inside these ranges and needn't reach their ends.
Inputs may be any that keep to these rules, and one draw needn't show every extreme that they name: `owner_map`: each owner is named by exactly one layer.
All inputs are finite; a program needn't handle non-finite values.
Results may differ from the reference program's by a relative error of at most 0.035.
Values may be sent and summed in bfloat16 or wider, within the bound.
No kernel may reach another device: no remote copies, remote signals or barrier semaphores. Data moves between devices by JAX's collectives and lax.ppermute only.
A program may use at most 128 MiB of HBM per device.

```python
import jax
import jax.numpy as jnp
from jax import lax

D = 8192
RANK = 64
LEN = 512
LAYERS = 4
TOKENS = 2048
NTRAIN = 4
NQ = 4096
N_TENSOR = 8
N_LAYER = 4


def levels(rng, extent, split, low, largest):
    def one(dim, shards_of):
        steps = jax.random.uniform(jax.random.fold_in(jax.random.fold_in(rng, 6), dim), (shards_of,), jnp.float32, low / len(split), largest / len(split))
        return jnp.repeat(jnp.exp(steps), extent[dim] // shards_of).reshape((-1,) + (1,) * (len(extent) - dim - 1))

    loudness = one(*split[0])
    for cut in split[1:]:
        loudness = loudness * one(*cut)
    return loudness


def scatter_about(key, shape, deviation, reach, shards=(), dtype=jnp.bfloat16):
    factor_of = levels(key, shape, shards, -0.22, 0.18) if shards else 1.0
    entries = jax.random.normal(key, shape, jnp.float32) * deviation * factor_of
    return jnp.minimum(jnp.maximum(entries, -reach), reach).astype(dtype)


def setup_inputs(seed: int = 0) -> dict:
    keys = jax.random.split(jax.random.key(seed), 8)
    return {
        "saved_inputs": scatter_about(keys[0], (LAYERS, TOKENS, D), 1.0, 6.0, ((1, 4), (2, 32))),
        "output_grad": scatter_about(keys[1], (TOKENS, D), 0.5, 4.0, ((0, 4), (1, 32))),
        "weights": scatter_about(keys[2], (LAYERS, D, N_TENSOR, N_LAYER, D // (N_TENSOR * N_LAYER)), D ** -0.5, 0.0625, ((1, 8), (3, 4))),
        "proj_in": scatter_about(keys[3], (LAYERS, RANK, D), D ** -0.5, 0.0625, ((2, 32),)),
        "proj_out": scatter_about(keys[4], (LAYERS, RANK, D), D ** -0.5, 0.0625, ((2, 32),)),
        "query_grads": scatter_about(keys[5], (LAYERS, NQ, RANK * RANK), (RANK * RANK * LEN) ** -0.5, 0.00390625, ((0, 4), (1, 32))),
        "owner_map": jax.random.permutation(keys[6], LAYERS).astype(jnp.int32),
    }


def reference(saved_inputs, output_grad, weights, proj_in, proj_out, query_grads, owner_map):
    layers = weights.shape[0]
    width = D // (N_TENSOR * N_LAYER)
    grad_now = output_grad.astype(jnp.float32)
    grad_bf = output_grad
    factors = [None] * layers
    for level in reversed(range(layers)):
        out_factor = jnp.dot(grad_bf, proj_out[level].T, preferred_element_type=jnp.float32)
        in_factor = jnp.dot(saved_inputs[level], proj_in[level].T, preferred_element_type=jnp.float32)
        factors[level] = (out_factor, in_factor)
        grid_grad = grad_bf.reshape(TOKENS, N_TENSOR, N_LAYER, width)
        summed = jnp.zeros((TOKENS, D), jnp.float32)
        for group in range(N_LAYER):
            columns = grid_grad[:, :, group, :].reshape(TOKENS, N_TENSOR * width)
            weight_cols = weights[level][:, :, group, :].reshape(D, N_TENSOR * width)
            term = lax.dot_general(columns, weight_cols, (((1,), (1,)), ((), ())), preferred_element_type=jnp.float32)
            rounded = lax.optimization_barrier(term.astype(jnp.bfloat16))
            summed = summed + rounded.astype(jnp.float32)
        grad_now = grad_now + summed
        grad_bf = grad_now.astype(jnp.bfloat16)
    scores = jnp.zeros((NTRAIN, NQ), jnp.float32)
    for level in range(layers):
        out_factor, in_factor = factors[level]
        left = out_factor.reshape(NTRAIN, LEN, RANK)
        right = in_factor.reshape(NTRAIN, LEN, RANK)
        blocks = jnp.einsum("eta,etb->eab", left, right, precision=lax.Precision.HIGHEST)
        blocks = blocks.reshape(NTRAIN, RANK * RANK).astype(jnp.bfloat16)
        queries = lax.dynamic_index_in_dim(query_grads, owner_map[level].astype(jnp.int32), 0, keepdims=False)
        scores = scores + lax.dot_general(blocks, queries, (((1,), (1,)), ((), ())), preferred_element_type=jnp.float32)
    return grad_bf, scores
```

```python
import jax
import jax.numpy as jnp
from jax import lax
from jax.experimental import pallas as pl
from jax.experimental.pallas import tpu as pltpu
from jax.sharding import PartitionSpec as P

NT = (((1,), (1,)), ((), ()))
F32 = jnp.float32
BF16 = jnp.bfloat16
VMEM_BYTES = 48 << 20


def features_first(weights, level, core):
    _, rows, cells, width = weights.shape
    step, half = 512, cells // 2

    def body(core_ref, w_ref, o_ref, s_ref):
        o_ref[...] = jnp.swapaxes(w_ref[0], 0, 1)
        s_ref[...] = o_ref[pl.ds(half * core_ref[0], half)]

    return pl.pallas_call(
        body,
        grid_spec=pltpu.PrefetchScalarGridSpec(
            num_scalar_prefetch=1,
            grid=(rows // step,),
            in_specs=[pl.BlockSpec((1, step, cells, width), lambda n, c: (level, n, 0, 0))],
            out_specs=[
                pl.BlockSpec((cells, step, width), lambda n, c: (0, n, 0)),
                pl.BlockSpec((half, step, width), lambda n, c: (0, n, 0)),
            ],
        ),
        out_shape=[
            jax.ShapeDtypeStruct((cells, rows, width), weights.dtype),
            jax.ShapeDtypeStruct((half, rows, width), weights.dtype),
        ],
        compiler_params=pltpu.CompilerParams(vmem_limit_bytes=VMEM_BYTES),
        cost_estimate=pl.CostEstimate(
            flops=0, bytes_accessed=5 * rows * cells * width, transcendentals=0
        ),
    )(core, weights)


def first_partial(gathered, weight):
    cells, tokens, width = gathered.shape
    rows = weight.shape[1]
    half = tokens // 2

    def body(g_ref, w_ref, o_ref):
        total = None
        for a in range(cells):
            term = lax.dot_general(g_ref[a], w_ref[a], NT, preferred_element_type=F32)
            total = term if total is None else total + term
        o_ref[0, 0] = total[:half].astype(o_ref.dtype)
        o_ref[1, 0] = total[half:].astype(o_ref.dtype)

    return pl.pallas_call(
        body,
        grid=(rows // width,),
        in_specs=[
            pl.BlockSpec((cells, tokens, width), lambda n: (0, 0, 0)),
            pl.BlockSpec((cells, width, width), lambda n: (0, n, 0)),
        ],
        out_specs=pl.BlockSpec((2, 1, half, width), lambda n: (0, n, 0, 0)),
        out_shape=jax.ShapeDtypeStruct((2, rows // width, half, width), BF16),
        compiler_params=pltpu.CompilerParams(vmem_limit_bytes=VMEM_BYTES),
        cost_estimate=pl.CostEstimate(
            flops=2 * cells * width * rows * tokens,
            bytes_accessed=2 * (cells * width * (rows + tokens) + rows * tokens),
            transcendentals=0,
        ),
    )(gathered, weight)


def pair_partial(place, gathered, own, near, far, kept=None):
    cells, tokens, width = gathered.shape
    rows = own.shape[1]
    groups = rows // width
    half = cells // 2
    last = kept is not None

    def body(s_ref, g_ref, own_ref, near_ref, far_ref, *refs):
        o_ref = refs[-1]
        phase, group = pl.program_id(0), pl.program_id(1)

        def put(total, column):
            if last:
                extra = refs[0][column]
                total = total + jnp.where(group == s_ref[2], extra, jnp.zeros_like(extra))
            o_ref[0, 0] = total.astype(o_ref.dtype)

        @pl.when(phase == 0)
        def _():
            total = None
            for a in range(cells):
                term = lax.dot_general(g_ref[a], own_ref[a], NT, preferred_element_type=F32)
                total = term if total is None else total + term
            put(total, s_ref[0])

        @pl.when(phase == 1)
        def _():
            total = None
            for ref, first in ((near_ref, s_ref[1]), (far_ref, 1 - s_ref[1])):
                for i in range(half):
                    term = lax.dot_general(
                        g_ref[half * first + i], ref[i], NT, preferred_element_type=F32
                    )
                    total = term if total is None else total + term
            put(total, 1 - s_ref[0])

    def column(p, s):
        return jnp.where(p == 0, s[0], 1 - s[0])

    if last:
        out_shape, out_map = (2, groups), lambda p, n, s: (column(p, s), n, 0, 0)
    else:
        out_shape, out_map = (groups, 2), lambda p, n, s: (n, column(p, s), 0, 0)
    in_specs = [
        pl.BlockSpec((cells, tokens, width), lambda p, n, s: (0, 0, 0)),
        pl.BlockSpec((cells, width, width), lambda p, n, s: (0, jnp.where(p == 0, n, groups - 1), 0)),
        pl.BlockSpec((half, width, width), lambda p, n, s: (0, jnp.where(p == 0, 0, n), 0)),
        pl.BlockSpec((half, width, width), lambda p, n, s: (0, jnp.where(p == 0, 0, n), 0)),
    ]
    operands = [gathered, own, near, far]
    if last:
        in_specs.append(pl.BlockSpec((2, tokens, width), lambda p, n, s: (0, 0, 0)))
        operands.append(kept)
    return pl.pallas_call(
        body,
        grid_spec=pltpu.PrefetchScalarGridSpec(
            num_scalar_prefetch=1,
            grid=(2, groups),
            in_specs=in_specs,
            out_specs=pl.BlockSpec((1, 1, tokens, width), out_map),
        ),
        out_shape=jax.ShapeDtypeStruct((*out_shape, tokens, width), BF16),
        compiler_params=pltpu.CompilerParams(vmem_limit_bytes=VMEM_BYTES),
        cost_estimate=pl.CostEstimate(
            flops=4 * cells * width * rows * tokens,
            bytes_accessed=2 * (cells * width * (2 * rows + tokens) + 2 * rows * tokens),
            transcendentals=0,
        ),
    )(place, *operands)


def exchange(blocks, axes, groups=None):
    return lax.all_to_all(blocks, axes, 0, 0, tiled=True, axis_index_groups=groups)


def spread(value, axes, peers, groups=None):
    return exchange(jnp.broadcast_to(value, (peers, *value.shape)), axes, groups)


def on_device(saved_inputs, output_grad, weights, proj_in, proj_out, query_grads, owner_map):
    layers, tokens, width = saved_inputs.shape
    rank = proj_in.shape[1]
    rows = weights.shape[1]
    n_dp, n_tensor, n_layer = (lax.axis_size(k) for k in ("dp", "tensor", "layer"))
    n_y = n_tensor // 2
    half = tokens // 2
    t, b = lax.axis_index("tensor"), lax.axis_index("layer")
    x, y = t % 2, t // 2
    core = lax.axis_index("dp") % 2
    place = jnp.stack([x, core, b]).astype(jnp.int32)
    core1 = core.astype(jnp.int32).reshape(1)
    along_y = [[2 * k + j for k in range(n_y)] for j in range(2)]
    along_xz = [[2 * n_layer * k + j for j in range(2 * n_layer)] for k in range(n_y)]
    across = [
        (d * n_tensor + k, (d ^ 2) * n_tensor + (k ^ 1)) for d in range(n_dp) for k in range(n_tensor)
    ]
    flat = weights.reshape(layers, rows, n_tensor, width)

    own, near, far = [None] * layers, [None] * layers, [None] * layers
    for level in (2, 3, 1, 0):
        own[level], passed = features_first(flat, level, core1)
        if level < layers - 1:
            near[level] = lax.ppermute(passed, ("dp", "tensor"), across)
            far[level] = lax.ppermute(near[level], "dp", [(d, d ^ 1) for d in range(n_dp)])
    other_proj = lax.ppermute(
        proj_out[: layers - 1], "tensor", [(k, k ^ 1) for k in range(n_tensor)]
    )
    pair_proj = jnp.where(
        x == 0, jnp.stack([proj_out[: layers - 1], other_proj]), jnp.stack([other_proj, proj_out[: layers - 1]])
    )

    outs = [None] * layers
    outs[layers - 1] = lax.dot_general(output_grad, proj_out[layers - 1], NT, preferred_element_type=F32)
    gathered = spread(output_grad, "tensor", n_tensor)
    partial = first_partial(gathered, own[layers - 1])
    arrived = exchange(partial.reshape(2 * n_layer, half, width), ("tensor", "layer"), along_xz)
    start = lax.dynamic_slice(
        gathered.reshape(n_y, 2, 2, half, width), (y, 0, x, 0, 0), (1, 2, 1, half, width)
    ).reshape(2, half, width)
    total = start.astype(F32) + arrived.reshape(2, n_layer, half, width).astype(F32).sum(axis=1)
    for level in reversed(range(layers - 1)):
        grad = total.astype(BF16)
        out_half = sum(
            lax.dot_general(grad[k], pair_proj[k, level], NT, preferred_element_type=F32)
            for k in range(2)
        )
        outs[level] = lax.dynamic_update_slice(jnp.zeros((tokens, rank), F32), out_half, (x * half, 0))
        gathered = spread(grad, "tensor", n_y, along_y).reshape(n_tensor, half, width)
        if level:
            partial = pair_partial(place, gathered, own[level], near[level], far[level])
            arrived = exchange(partial, "layer")
            total = total + arrived.astype(F32).sum(axis=0)
        else:
            partial = pair_partial(place, gathered, own[level], near[level], far[level], total)
            arrived = exchange(
                partial.reshape(2 * n_layer, half, width), ("tensor", "layer"), along_xz
            )
            total = arrived.reshape(2, n_layer, half, width).astype(F32).sum(axis=1)
    input_grad = total.astype(BF16).reshape(tokens, width)

    stacked = jnp.stack(
        [
            jnp.concatenate(
                [
                    outs[k],
                    lax.dot_general(saved_inputs[k], proj_in[k], NT, preferred_element_type=F32),
                ],
                axis=1,
            )
            for k in range(layers)
        ]
    ).astype(BF16)
    owners = jnp.arange(n_layer, dtype=jnp.int32)
    inverse = jnp.sum(
        owners[None, :] * (owner_map[None, :] == owners[:, None]).astype(jnp.int32), axis=1
    )
    block_rows = tokens // n_tensor
    by_owner = jnp.take(stacked, inverse, axis=0).reshape(n_layer, n_tensor, block_rows, 2 * rank)
    ordered = jnp.swapaxes(by_owner, 0, 1).reshape(n_tensor * n_layer, block_rows, 2 * rank)
    mine = exchange(ordered, ("tensor", "layer")).astype(F32).sum(axis=0)
    block = lax.dot_general(
        mine[:, :rank], mine[:, rank:], (((0,), (0,)), ((), ())),
        preferred_element_type=F32, precision=lax.Precision.HIGHEST,
    ).reshape(rank * rank)
    every = spread(block, ("dp", "tensor"), n_dp * n_tensor)
    whole = every.reshape(n_dp, n_tensor, rank * rank).sum(axis=1).astype(BF16)
    scored = lax.dot_general(whole, query_grads[0], NT, preferred_element_type=F32)
    scores = exchange(scored, "layer").sum(axis=0, keepdims=True)
    return input_grad, scores


def solution(mesh):
    in_specs = (
        P(None, "dp", ("tensor", "layer")),
        P("dp", ("tensor", "layer")),
        P(None, "tensor", None, "layer", None),
        P(None, None, ("tensor", "layer")),
        P(None, None, ("tensor", "layer")),
        P("layer", ("dp", "tensor"), None),
        P(),
    )
    out_specs = (P("dp", ("tensor", "layer")), P("layer", ("dp", "tensor")))
    return jax.shard_map(
        on_device, mesh=mesh, in_specs=in_specs, out_specs=out_specs, check_vma=False
    )
```

```python
import jax
import jax.numpy as jnp
from jax import lax
from jax.experimental import pallas as pl
from jax.experimental.pallas import tpu as pltpu
from jax.sharding import PartitionSpec as P

NT = (((1,), (1,)), ((), ()))
F32 = jnp.float32
BF16 = jnp.bfloat16
WIDE = pl.BlockSpec(memory_space=pltpu.VMEM)
SCALARS = pl.BlockSpec(memory_space=pltpu.SMEM)
after = lax.optimization_barrier


def limit(mib):
    return pltpu.CompilerParams(vmem_limit_bytes=mib << 20)


def features_first(weights, level, core):
    _, rows, cells, width = weights.shape
    step, half = 512, cells // 2

    def body(core_ref, w_ref, o_ref, s_ref):
        o_ref[...] = jnp.swapaxes(w_ref[0], 0, 1)
        s_ref[...] = o_ref[pl.ds(half * core_ref[0], half)]

    return pl.pallas_call(
        body,
        grid_spec=pltpu.PrefetchScalarGridSpec(
            num_scalar_prefetch=1,
            grid=(rows // step,),
            in_specs=[pl.BlockSpec((1, step, cells, width), lambda n, c: (level, n, 0, 0))],
            out_specs=[
                pl.BlockSpec((cells, step, width), lambda n, c: (0, n, 0)),
                pl.BlockSpec((half, step, width), lambda n, c: (0, n, 0)),
            ],
        ),
        out_shape=[
            jax.ShapeDtypeStruct((cells, rows, width), weights.dtype),
            jax.ShapeDtypeStruct((half, rows, width), weights.dtype),
        ],
        compiler_params=limit(20),
        cost_estimate=pl.CostEstimate(
            flops=0, bytes_accessed=5 * rows * cells * width, transcendentals=0
        ),
    )(core, weights)


def first_partial(gathered, weight, extra):
    cells, tokens, width = gathered.shape
    rows = weight.shape[1]
    groups = rows // width
    half = tokens // 2
    tail = extra.shape[1]

    def body(g_ref, w_ref, e_ref, o_ref):
        for n in range(groups):
            total = None
            for a in range(cells):
                term = lax.dot_general(
                    g_ref[a], w_ref[a, n * width : (n + 1) * width], NT,
                    preferred_element_type=F32,
                )
                total = term if total is None else total + term
            o_ref[n, :half] = total[:half].astype(o_ref.dtype)
            o_ref[groups + n, :half] = total[half:].astype(o_ref.dtype)
        o_ref[:, half:] = e_ref[...]

    return pl.pallas_call(
        body,
        in_specs=[WIDE, WIDE, WIDE],
        out_specs=WIDE,
        out_shape=jax.ShapeDtypeStruct((2 * groups, half + tail, width), BF16),
        compiler_params=limit(16),
        cost_estimate=pl.CostEstimate(
            flops=2 * cells * width * rows * tokens,
            bytes_accessed=2 * (cells * width * (rows + tokens) + rows * tokens),
            transcendentals=0,
        ),
    )(gathered, weight, extra)


def pair_partial(place, gathered, own, near, far, kept=None, extra=None):
    n_y, _, width = gathered.shape
    cells, rows, _ = own.shape
    tokens = width
    groups = rows // width
    half = cells // 2
    last = kept is not None
    tail = 0 if extra is None else extra.shape[1]
    operands = [gathered, own, near, far]
    operands += [kept] if last else []
    operands += [] if extra is None else [extra]
    blocks, deep = (2 * groups, tokens) if last else (groups, 2 * tokens)

    def body(s_ref, g_ref, own_ref, near_ref, far_ref, *refs):
        o_ref = refs[-1]
        x, core, b = s_ref[0], s_ref[1], s_ref[2]

        def piece(cell):
            return g_ref[cell // 2, (cell % 2) * tokens : (cell % 2 + 1) * tokens]

        def put(total, column, n):
            if last:
                mine = refs[0][column]
                total = total + jnp.where(n == b, mine, jnp.zeros_like(mine))
                o_ref[groups * column + n, :tokens] = total.astype(o_ref.dtype)
            else:
                start = pl.multiple_of(column * tokens, tokens)
                o_ref[n, pl.ds(start, tokens)] = total.astype(o_ref.dtype)

        for n in range(groups):
            cut = slice(n * width, (n + 1) * width)
            total = None
            for a in range(cells):
                term = lax.dot_general(
                    piece(a), own_ref[a, cut], NT, preferred_element_type=F32
                )
                total = term if total is None else total + term
            put(total, x, n)
        for n in range(groups):
            cut = slice(n * width, (n + 1) * width)
            total = None
            for ref, first in ((near_ref, core), (far_ref, 1 - core)):
                for i in range(half):
                    values = g_ref[
                        (half // 2) * first + i // 2, (i % 2) * tokens : (i % 2 + 1) * tokens
                    ]
                    term = lax.dot_general(
                        values, ref[i, cut], NT, preferred_element_type=F32
                    )
                    total = term if total is None else total + term
            put(total, 1 - x, n)
        if tail:
            for k in range(blocks):
                o_ref[k, deep:] = refs[-2][k % extra.shape[0]]

    return pl.pallas_call(
        body,
        in_specs=[SCALARS] + [WIDE] * len(operands),
        out_specs=WIDE,
        out_shape=jax.ShapeDtypeStruct((blocks, deep + tail, width), BF16),
        compiler_params=limit(16),
        cost_estimate=pl.CostEstimate(
            flops=4 * cells * width * rows * tokens,
            bytes_accessed=2 * (cells * width * (2 * rows + tokens) + 2 * rows * tokens),
            transcendentals=0,
        ),
    )(place, *operands)


def out_factors(grad, proj):
    def body(g_ref, p_ref, o_ref):
        total = lax.dot_general(p_ref[0], g_ref[0], NT, preferred_element_type=F32)
        total += lax.dot_general(p_ref[1], g_ref[1], NT, preferred_element_type=F32)
        o_ref[...] = total.astype(o_ref.dtype)

    return pl.pallas_call(
        body,
        in_specs=[WIDE, WIDE],
        out_specs=WIDE,
        out_shape=jax.ShapeDtypeStruct((proj.shape[1], grad.shape[1]), BF16),
        compiler_params=limit(8),
    )(grad, proj)


def block_parts(layer_of, outs, ins):
    layers, rank, tokens = outs.shape
    low = rank // 2

    def body(l_ref, a_ref, b_ref, o_ref):
        for o in range(layers):
            part = lax.dot_general(
                a_ref[l_ref[o]], b_ref[l_ref[o]], NT, preferred_element_type=F32
            ).astype(o_ref.dtype)
            side = jnp.concatenate([part[:low], part[low:]], axis=1)
            row, lane = low * (o // 2), 2 * rank * (o % 2)
            o_ref[row : row + low, lane : lane + 2 * rank] = side

    return pl.pallas_call(
        body,
        in_specs=[SCALARS, WIDE, WIDE],
        out_specs=WIDE,
        out_shape=jax.ShapeDtypeStruct((low * layers // 2, 4 * rank), BF16),
        compiler_params=limit(8),
    )(layer_of, outs, ins)


def exchange(blocks, axes, groups=None):
    return lax.all_to_all(blocks, axes, 0, 0, tiled=True, axis_index_groups=groups)


def spread(value, axes, peers, groups=None):
    return exchange(jnp.broadcast_to(value, (peers, *value.shape)), axes, groups)


def on_device(saved_inputs, output_grad, weights, proj_in, proj_out, query_grads, owner_map):
    layers, tokens, width = saved_inputs.shape
    rank = proj_in.shape[1]
    rows = weights.shape[1]
    n_dp, n_tensor, n_layer = (lax.axis_size(k) for k in ("dp", "tensor", "layer"))
    n_y = n_tensor // 2
    half = tokens // 2
    t, b = lax.axis_index("tensor"), lax.axis_index("layer")
    x, y = t % 2, t // 2
    core = lax.axis_index("dp") % 2
    place = jnp.stack([x, core, b]).astype(jnp.int32)
    along_y = [[2 * k + j for k in range(n_y)] for j in range(2)]
    along_xz = [[2 * n_layer * k + j for j in range(2 * n_layer)] for k in range(n_y)]
    within_y = [
        [
            (d * n_tensor + 2 * k + j) * n_layer + z
            for d in range(n_dp)
            for j in range(2)
            for z in range(n_layer)
        ]
        for k in range(n_y)
    ]
    across = [
        (d * n_tensor + k, (d ^ 2) * n_tensor + (k ^ 1)) for d in range(n_dp) for k in range(n_tensor)
    ]
    beside = [(k, k ^ 1) for k in range(n_tensor)]
    other_core = [(d, d ^ 1) for d in range(n_dp)]
    flat = pltpu.with_memory_space_constraint(
        weights.reshape(layers, rows, n_tensor, width), pltpu.HBM
    )
    top = layers - 1
    owners = jnp.arange(n_layer, dtype=jnp.int32)
    layer_of = jnp.sum(
        owners[None, :] * (owner_map[None, :] == owners[:, None]).astype(jnp.int32), axis=1
    )

    gathered = spread(output_grad, "tensor", n_tensor)
    own, passed, near, far = ([None] * layers for _ in range(4))
    for level in (2, 3, 1, 0):
        own[level], passed[level] = features_first(flat, level, core.astype(jnp.int32).reshape(1))
    near[2] = lax.ppermute(passed[2], ("dp", "tensor"), across)
    other_proj = lax.ppermute(proj_out, "tensor", beside)
    pair_proj = jnp.where(
        x == 0, jnp.stack([proj_out, other_proj], 1), jnp.stack([other_proj, proj_out], 1)
    )
    in_parts = jnp.stack(
        [
            lax.dot_general(proj_in[k], saved_inputs[k], NT, preferred_element_type=F32).astype(BF16)
            for k in range(layers)
        ]
    )
    in_parts = jnp.swapaxes(in_parts.reshape(layers, rank, 2, half), 1, 2)
    in_parts = jnp.swapaxes(in_parts, 0, 1).reshape(2 * layers, rank, half)

    partial = first_partial(gathered, own[top], in_parts)
    arrived = exchange(partial, ("tensor", "layer"), along_xz)
    arrived = arrived.reshape(2, n_layer, half + rank, width)
    start = lax.dynamic_slice(
        gathered.reshape(n_y, 2, 2, half, width), (y, 0, x, 0, 0), (1, 2, 1, half, width)
    ).reshape(2, half, width)
    total = start.astype(F32) + arrived[:, :, :half].astype(F32).sum(axis=1)
    in_mine = arrived[:, :, half:].astype(F32).sum(axis=(0, 1)).astype(BF16)
    grad = total.astype(BF16)
    outs = [None] * layers
    outs[3] = out_factors(start, pair_proj[3])

    outs[2] = out_factors(grad, pair_proj[2])
    grad, outs[2], outs[3] = after((grad, outs[2], outs[3]))
    passed[1], _ = after((passed[1], grad))
    near[1] = lax.ppermute(passed[1], "tensor", beside)
    near[2], _ = after((near[2], grad))
    far[2] = lax.ppermute(near[2], "dp", other_core)
    passed[0], _ = after((passed[0], near[2]))
    near[0] = lax.ppermute(passed[0], ("dp", "tensor"), across)
    gathered = spread(
        jnp.concatenate([grad.reshape(2 * half, width), in_mine]), "tensor", n_y, along_y
    )
    in_whole = gathered[:, 2 * half :].astype(F32).sum(axis=0).astype(BF16)
    partial = pair_partial(
        place, gathered, own[2], near[2], far[2], extra=in_whole.reshape(1, rank, half)
    )
    arrived = exchange(partial, "layer")
    ins = arrived[:, 2 * half :]
    total = total + arrived[:, : 2 * half].astype(F32).sum(axis=0).reshape(2, half, width)
    grad = total.astype(BF16)

    outs[1] = out_factors(grad, pair_proj[1])
    grad, outs[1] = after((grad, outs[1]))
    gathered = spread(grad.reshape(2 * half, width), "tensor", n_y, along_y)
    near[1], _ = after((near[1], gathered))
    far[1] = lax.ppermute(near[1], "dp", other_core)
    partial = pair_partial(place, gathered, own[1], near[1], far[1])
    near[0], _ = after((near[0], partial))
    far[0] = lax.ppermute(near[0], "dp", other_core)
    arrived = exchange(partial, "layer")
    total = total + arrived.astype(F32).sum(axis=0).reshape(2, half, width)
    grad = total.astype(BF16)

    outs[0] = out_factors(grad, pair_proj[0])
    blocks = block_parts(layer_of, jnp.stack(outs), ins)
    gathered = spread(
        jnp.concatenate([grad.reshape(2 * half, width), blocks]), "tensor", n_y, along_y
    )
    summed = gathered[:, 2 * half :].astype(F32).sum(axis=0).astype(BF16)
    summed = jnp.swapaxes(summed.reshape(2, rank // 2, 2, 2 * rank), 1, 2)
    summed = summed.reshape(n_layer, rank // 2, 2 * rank)
    every = exchange(
        jnp.broadcast_to(summed, (n_dp * 2, *summed.shape)).reshape(
            n_dp * 2 * n_layer, rank // 2, 2 * rank
        ),
        ("dp", "tensor", "layer"),
        within_y,
    )
    whole = every.reshape(n_dp, 2 * n_layer, rank // 2, 2, rank).astype(F32).sum(axis=1)
    whole = jnp.swapaxes(whole, 1, 2).reshape(n_dp, rank * rank).astype(BF16)
    scored = lax.dot_general(whole, query_grads[0], NT, preferred_element_type=F32)
    high = scored.astype(BF16)
    low = (scored - high.astype(F32)).astype(BF16)
    carried = jnp.concatenate([high, low], axis=1)[:, None, :]
    carried = jnp.broadcast_to(carried, (n_dp, 16, width))
    partial = pair_partial(place, gathered, own[0], near[0], far[0], kept=total, extra=carried)
    arrived = exchange(partial, ("tensor", "layer"), along_xz)
    arrived = arrived.reshape(2, n_layer, half + 16, width)
    input_grad = arrived[:, :, :half].astype(F32).sum(axis=1).astype(BF16).reshape(tokens, width)
    ends = lax.dynamic_index_in_dim(arrived[:, :, half], x, 0, keepdims=False).astype(F32).sum(axis=0)
    scores = (ends[: width // 2] + ends[width // 2 :])[None]
    return input_grad, scores


def solution(mesh):
    in_specs = (
        P(None, "dp", ("tensor", "layer")),
        P("dp", ("tensor", "layer")),
        P(None, "tensor", None, "layer", None),
        P(None, None, ("tensor", "layer")),
        P(None, None, ("tensor", "layer")),
        P("layer", ("dp", "tensor"), None),
        P(),
    )
    out_specs = (P("dp", ("tensor", "layer")), P("layer", ("dp", "tensor")))
    return jax.shard_map(
        on_device, mesh=mesh, in_specs=in_specs, out_specs=out_specs, check_vma=False
    )
```

```python
import jax
import jax.numpy as jnp
from jax import lax
from jax.experimental import pallas as pl
from jax.experimental.pallas import tpu as pltpu
from jax.sharding import PartitionSpec as P

NT = (((1,), (1,)), ((), ()))
NN = (((1,), (0,)), ((), ()))
F32 = jnp.float32
BF16 = jnp.bfloat16
WIDE = pl.BlockSpec(memory_space=pltpu.VMEM)
SCALARS = pl.BlockSpec(memory_space=pltpu.SMEM)
after = lax.optimization_barrier


def limit(mib):
    return pltpu.CompilerParams(vmem_limit_bytes=mib << 20)


def dot(left, right, dims=NN):
    return lax.dot_general(left, right, dims, preferred_element_type=F32)


def sum_of(terms):
    total = None
    for term in terms:
        total = term if total is None else total + term
    return total


def local_call(body, outs, operands, scalars=(), cost=None):
    return pl.pallas_call(
        body,
        in_specs=[SCALARS] * len(scalars) + [WIDE] * len(operands),
        out_specs=[WIDE] * len(outs),
        out_shape=[jax.ShapeDtypeStruct(*out) for out in outs],
        compiler_params=limit(8),
        cost_estimate=cost,
    )(*scalars, *operands)


def features_first(weights, levels, core, pieces):
    _, rows, cells, width = weights.shape
    step, half = 512, cells // 2
    steps = rows // step
    count = len(levels)
    deep = half // max(pieces, 1)

    def body(core_ref, w_ref, *refs):
        own_refs, s_refs = refs[:count], refs[count:]
        for k, o_ref in enumerate(own_refs):

            @pl.when(pl.program_id(0) == k)
            def _(o_ref=o_ref):
                o_ref[...] = jnp.swapaxes(w_ref[0], 0, 1)
                for i, s_ref in enumerate(s_refs):
                    s_ref[0] = o_ref[pl.ds(half * core_ref[0] + deep * i, deep)]

    def own_map(k):
        def index(m, n, c):
            return (0, jnp.where(m < k, 0, jnp.where(m > k, steps - 1, n)), 0)

        return index

    return pl.pallas_call(
        body,
        grid_spec=pltpu.PrefetchScalarGridSpec(
            num_scalar_prefetch=1,
            grid=(count, steps),
            in_specs=[
                pl.BlockSpec(
                    (1, step, cells, width), lambda m, n, c: (levels[0] - m, n, 0, 0)
                )
            ],
            out_specs=[pl.BlockSpec((cells, step, width), own_map(k)) for k in range(count)]
            + [pl.BlockSpec((1, deep, step, width), lambda m, n, c: (m, 0, n, 0))] * pieces,
        ),
        out_shape=[jax.ShapeDtypeStruct((cells, rows, width), weights.dtype)] * count
        + [jax.ShapeDtypeStruct((count, deep, rows, width), weights.dtype)] * pieces,
        compiler_params=limit(14 + 6 * (count - 1)),
        cost_estimate=pl.CostEstimate(
            flops=0, bytes_accessed=5 * count * rows * cells * width, transcendentals=0
        ),
    )(core, weights)


def first_partial(gathered, weight, extra):
    cells, tokens, width = gathered.shape
    rows = weight.shape[1]
    groups = rows // width
    half = tokens // 2
    tail = extra.shape[1]

    def body(g_ref, w_ref, e_ref, o_ref):
        for h in range(2):
            for n in range(groups):
                total = sum_of(
                    dot(
                        w_ref[a, n * width : (n + 1) * width],
                        g_ref[a, h * half : (h + 1) * half],
                        NT,
                    )
                    for a in range(cells)
                )
                o_ref[h * groups + n, :width] = total.astype(o_ref.dtype)
        o_ref[:, width:] = e_ref[...]

    return local_call(
        body,
        [((2 * groups, width + tail, half), BF16)],
        [gathered, weight, extra],
        cost=pl.CostEstimate(
            flops=2 * cells * width * rows * tokens,
            bytes_accessed=2 * (cells * width * (rows + tokens) + rows * tokens),
            transcendentals=0,
        ),
    )[0]


def pair_totals(s_ref, g_ref, w_refs, slot, groups):
    own_ref, *others = w_refs
    cells, _, width = own_ref.shape
    half = cells // 2
    deep = others[0].shape[1]
    pieces = half // deep
    x, core = s_ref[0], s_ref[1]
    for n in range(groups):
        cut = slice(n * width, (n + 1) * width)
        yield x, n, sum_of(
            dot(own_ref[a, cut], g_ref[a // 2, (a % 2) * width : (a % 2 + 1) * width])
            for a in range(cells)
        )
    for n in range(groups):
        cut = slice(n * width, (n + 1) * width)
        yield 1 - x, n, sum_of(
            dot(
                refs[i // deep][slot, i % deep, cut],
                g_ref[(half // 2) * first + i // 2, (i % 2) * width : (i % 2 + 1) * width],
            )
            for first, refs in ((core, others[:pieces]), (1 - core, others[pieces:]))
            for i in range(half)
        )


def pair_cost(own, tokens):
    cells, rows, width = own.shape
    return pl.CostEstimate(
        flops=4 * cells * width * rows * tokens,
        bytes_accessed=4 * cells * width * rows,
        transcendentals=0,
    )


def pair_partial(place, gathered, held, slot, extra):
    own = held[0]
    width = own.shape[2]
    groups = own.shape[1] // width

    def body(s_ref, g_ref, *refs):
        *w_refs, e_ref, o_ref = refs
        for column, n, total in pair_totals(s_ref, g_ref, w_refs, slot, groups):
            start = pl.multiple_of(column * width, width)
            o_ref[n, pl.ds(start, width)] = total.astype(o_ref.dtype)
        for n in range(groups):
            o_ref[n, 2 * width :] = e_ref[...]

    return local_call(
        body,
        [((groups, 2 * width + extra.shape[0], gathered.shape[2]), BF16)],
        [gathered, *held, extra],
        [place],
        pair_cost(own, gathered.shape[2]),
    )[0]


def pair_partial_scored(place, layer_of, gathered, held, slot, outs, kept_out, proj, ins):
    own = held[0]
    width = own.shape[2]
    groups = own.shape[1] // width
    rank = ins.shape[1]
    quarter = rank // 4

    def body(s_ref, l_ref, g_ref, *refs):
        *w_refs, a_ref, k_ref, p_ref, i_ref, o_ref, f_ref = refs
        f_ref[1:] = a_ref[...]
        final = k_ref[...]
        for column, n, total in pair_totals(s_ref, g_ref, w_refs, slot, groups):
            start = pl.multiple_of(column * width, width)
            rounded = total.astype(o_ref.dtype)
            o_ref[n, pl.ds(start, width)] = rounded
            final = final + dot(p_ref[n, column], rounded)
        f_ref[0] = final.astype(f_ref.dtype)
        for o in range(groups):
            block = dot(f_ref[l_ref[o]], i_ref[l_ref[o]], NT).astype(o_ref.dtype)
            o_ref[o, 2 * width :] = jnp.concatenate(
                [block[quarter * j : quarter * (j + 1)] for j in range(4)], axis=1
            )

    tokens = gathered.shape[2]
    return local_call(
        body,
        [((groups, 2 * width + quarter, tokens), BF16), ((outs.shape[0] + 1, rank, tokens), BF16)],
        [gathered, *held, outs, kept_out, proj, ins],
        [place, layer_of],
        pair_cost(own, tokens),
    )[0]


def last_partial(place, gathered, held, slot, kept, extra):
    own = held[0]
    width = own.shape[2]
    groups = own.shape[1] // width

    def body(s_ref, g_ref, *refs):
        *w_refs, t_ref, e_ref, o_ref = refs
        for column, n, total in pair_totals(s_ref, g_ref, w_refs, slot, groups):
            start = pl.multiple_of(column * width, width)
            mine = t_ref[pl.ds(start, width)]
            total = total + jnp.where(n == s_ref[2], mine, jnp.zeros_like(mine))
            o_ref[groups * column + n, :width] = total.astype(o_ref.dtype)
        for k in range(2 * groups):
            o_ref[k, width:] = e_ref[k % groups]

    return local_call(
        body,
        [((2 * groups, width + extra.shape[1], gathered.shape[2]), BF16)],
        [gathered, *held, kept, extra],
        [place],
        pair_cost(own, gathered.shape[2]),
    )[0]


def settle_first(place, arrived, gathered, proj_top, proj_next):
    blocks, deep, half = arrived.shape
    width = gathered.shape[2]
    groups = blocks // 2
    rank = proj_top.shape[1]

    def body(s_ref, r_ref, g_ref, p_ref, q_ref, t_ref, c_ref, o_ref):
        x, y = s_ref[0], s_ref[3]
        outs = [None, None]
        for k in range(2):
            start = g_ref[2 * y + k, pl.ds(pl.multiple_of(x * half, half), half)].astype(F32).T
            outs[0] = sum_of([*([outs[0]] if k else []), dot(p_ref[k], start.astype(BF16))])
            total = start + sum_of(r_ref[groups * k + z, :width].astype(F32) for z in range(groups))
            t_ref[k * width : (k + 1) * width] = total
            rounded = total.astype(BF16)
            outs[1] = sum_of([*([outs[1]] if k else []), dot(q_ref[k], rounded)])
            for j in range(c_ref.shape[0]):
                c_ref[j, k * width : (k + 1) * width] = rounded
        ins = sum_of(r_ref[k, width:].astype(F32) for k in range(blocks)).astype(BF16)
        for j in range(c_ref.shape[0]):
            c_ref[j, 2 * width :] = ins
        o_ref[0] = outs[0].astype(BF16)
        o_ref[1] = outs[1].astype(BF16)

    return local_call(
        body,
        [
            ((2 * width, half), F32),
            ((gathered.shape[0] // 2, 2 * width + deep - width, half), BF16),
            ((2, rank, half), BF16),
        ],
        [arrived, gathered, proj_top, proj_next],
        [place],
    )


def settle(arrived, total, projs):
    groups, _, half = arrived.shape
    depth = total.shape[0]
    width = depth // 2
    count, _, rank, _ = projs.shape

    def body(r_ref, t_ref, p_ref, o_ref, c_ref, f_ref):
        value = t_ref[...] + sum_of(r_ref[z, :depth].astype(F32) for z in range(groups))
        o_ref[...] = value
        rounded = value.astype(BF16)
        for j in range(c_ref.shape[0]):
            c_ref[j] = rounded
        for i in range(count):
            f_ref[i] = dot(p_ref[i, 0], rounded[:width]) + dot(p_ref[i, 1], rounded[width:])

    return local_call(
        body,
        [(total.shape, F32), ((groups, depth, half), BF16), ((count, rank, half), F32)],
        [arrived, total, projs],
    )


def settle_scored(arrived, total):
    groups, deep, half = arrived.shape
    depth = total.shape[0]

    def body(r_ref, t_ref, o_ref, c_ref):
        value = t_ref[...] + sum_of(r_ref[z, :depth].astype(F32) for z in range(groups))
        o_ref[...] = value
        rounded = value.astype(BF16)
        blocks = sum_of(r_ref[z, depth:].astype(F32) for z in range(groups)).astype(BF16)
        for j in range(c_ref.shape[0]):
            c_ref[j, :depth] = rounded
            c_ref[j, depth:] = blocks

    return local_call(
        body, [(total.shape, F32), ((groups, deep, half), BF16)], [arrived, total]
    )


def finish(arrived):
    blocks, _, half = arrived.shape
    groups = blocks // 2
    width = half

    def body(r_ref, o_ref):
        for k in range(2):
            value = sum_of(r_ref[groups * k + z, :width].astype(F32) for z in range(groups))
            o_ref[k * half : (k + 1) * half] = value.T.astype(o_ref.dtype)

    return local_call(body, [((2 * half, width), BF16)], [arrived])[0]


def exchange(blocks, axes, groups=None):
    return lax.all_to_all(blocks, axes, 0, 0, tiled=True, axis_index_groups=groups)


def on_device(saved_inputs, output_grad, weights, proj_in, proj_out, query_grads, owner_map):
    layers, tokens, width = saved_inputs.shape
    rank = proj_in.shape[1]
    rows = weights.shape[1]
    n_dp, n_tensor, n_layer = (lax.axis_size(k) for k in ("dp", "tensor", "layer"))
    n_y = n_tensor // 2
    half = tokens // 2
    t, b = lax.axis_index("tensor"), lax.axis_index("layer")
    x, y = t & 1, t >> 1
    core = lax.axis_index("dp") & 1
    place = jnp.stack([x, core, b, y]).astype(jnp.int32)
    along_y = [[2 * k + j for k in range(n_y)] for j in range(2)]
    along_xz = [[2 * n_layer * k + j for j in range(2 * n_layer)] for k in range(n_y)]
    along_dp_x = [
        [d * n_tensor + 2 * k + j for d in range(n_dp) for j in range(2)] for k in range(n_y)
    ]
    across = [
        (d * n_tensor + k, (d ^ 2) * n_tensor + (k ^ 1)) for d in range(n_dp) for k in range(n_tensor)
    ]
    beside = [(k, k ^ 1) for k in range(n_tensor)]
    to_other_core = [(d, d ^ 1) for d in range(n_dp)]
    flat = pltpu.with_memory_space_constraint(
        weights.reshape(layers, rows, n_tensor, width), pltpu.HBM
    )
    owners = jnp.arange(n_layer, dtype=jnp.int32)
    layer_of = jnp.sum(
        owners[None, :] * (owner_map[None, :] == owners[:, None]).astype(jnp.int32), axis=1
    )

    gathered = exchange(
        jnp.broadcast_to(output_grad, (n_tensor, *output_grad.shape)), "tensor"
    )
    one = core.astype(jnp.int32).reshape(1)
    own = [None] * layers
    own[2], passed_first = features_first(flat, [2], one, 1)
    near_first = lax.ppermute(passed_first, ("dp", "tensor"), across)
    (own[3],) = features_first(flat, [3], one, 0)
    own[1], own[0], *passed = features_first(flat, [1, 0], one, 2)
    other_proj = lax.ppermute(proj_out, "tensor", beside)
    pair_proj = jnp.where(
        x == 0, jnp.stack([proj_out, other_proj], 1), jnp.stack([other_proj, proj_out], 1)
    )
    shifted = [pair_proj[0]] + [
        lax.ppermute(pair_proj[0], "layer", [(z, z ^ k) for z in range(n_layer)])
        for k in range(1, n_layer)
    ]
    last_proj = jnp.stack(
        [
            sum_of(jnp.where((b ^ k) == z, shifted[k], 0) for k in range(n_layer))
            for z in range(n_layer)
        ]
    ).astype(BF16)
    in_parts = jnp.stack(
        [dot(proj_in[k], saved_inputs[k], NT).astype(BF16) for k in range(layers)]
    )
    in_parts = jnp.stack([in_parts[:, :, :half], in_parts[:, :, half:]])
    in_parts = in_parts.reshape(2 * layers, rank, half)
    gathered, own, passed, pair_proj, last_proj, in_parts = after(
        (gathered, own, passed, pair_proj, last_proj, in_parts)
    )

    partial = first_partial(gathered, own[3], in_parts)
    arrived = exchange(partial, ("tensor", "layer"), along_xz)
    total, copies, outs_top = settle_first(place, arrived, gathered, pair_proj[3], pair_proj[2])

    passed, _ = after((passed, total))
    near = [
        lax.ppermute(passed[0], ("dp", "tensor"), across),
        lax.ppermute(passed[1], "tensor", beside),
    ]
    near_first, _ = after((near_first, total))
    far_first = lax.ppermute(near_first, "dp", to_other_core)
    gathered = exchange(copies, "tensor", along_y)
    in_whole = gathered[:, 2 * width :].astype(F32).sum(axis=0).astype(BF16)
    partial = pair_partial(place, gathered, [own[2], near_first, far_first], 0, in_whole)
    arrived = exchange(partial, "layer")
    ins = arrived[:, 2 * width :]
    total, copies, outs_low = settle(arrived, total, jnp.stack([pair_proj[1], pair_proj[0]]))
    outs = jnp.stack([outs_low[0].astype(BF16), outs_top[1], outs_top[0]])
    copies, outs, ins = after((copies, outs, ins))

    gathered = exchange(copies, "tensor", along_y)
    near, _ = after((near, copies))
    far = [lax.ppermute(v, "dp", to_other_core) for v in near]
    partial = pair_partial_scored(
        place, layer_of, gathered, [own[1], *near, *far], 0, outs, outs_low[1], last_proj, ins
    )
    arrived = exchange(partial, "layer")
    total, copies = settle_scored(arrived, total)

    gathered = exchange(copies, "tensor", along_y)
    summed = gathered[:, 2 * width :].astype(F32).sum(axis=0).astype(BF16)
    every = exchange(
        jnp.broadcast_to(summed, (2 * n_dp, *summed.shape)), ("dp", "tensor"), along_dp_x
    )
    whole = every.reshape(n_dp, 2, rank // 4, 4, rank).astype(F32).sum(axis=1)
    whole = jnp.swapaxes(whole, 1, 2).reshape(n_dp, rank * rank).astype(BF16)
    scored = dot(whole, query_grads[0], NT)
    high = scored.astype(BF16)
    low = (scored - high.astype(F32)).astype(BF16)
    carried = jnp.concatenate([high, low], axis=1)[:, None, :]
    carried = jnp.broadcast_to(carried, (n_dp, 16, carried.shape[2]))
    partial = last_partial(place, gathered, [own[0], *near, *far], 1, total, carried)
    arrived = exchange(partial, ("tensor", "layer"), along_xz)
    input_grad = finish(arrived)
    ends = arrived.reshape(2, n_layer, *arrived.shape[1:])[:, :, width]
    ends = lax.dynamic_index_in_dim(ends, x, 0, keepdims=False).astype(F32).sum(axis=0)
    scores = (ends[: ends.shape[0] // 2] + ends[ends.shape[0] // 2 :])[None]
    return input_grad, scores


def solution(mesh):
    in_specs = (
        P(None, "dp", ("tensor", "layer")),
        P("dp", ("tensor", "layer")),
        P(None, "tensor", None, "layer", None),
        P(None, None, ("tensor", "layer")),
        P(None, None, ("tensor", "layer")),
        P("layer", ("dp", "tensor"), None),
        P(),
    )
    out_specs = (P("dp", ("tensor", "layer")), P("layer", ("dp", "tensor")))
    return jax.shard_map(
        on_device, mesh=mesh, in_specs=in_specs, out_specs=out_specs, check_vma=False
    )
```

```python
import jax
import jax.numpy as jnp
from jax import lax
from jax.experimental import pallas as pl
from jax.experimental.pallas import tpu as pltpu
from jax.sharding import PartitionSpec as P

NT = (((1,), (1,)), ((), ()))
NN = (((1,), (0,)), ((), ()))
F32 = jnp.float32
BF16 = jnp.bfloat16
WIDE = pl.BlockSpec(memory_space=pltpu.VMEM)
SCALARS = pl.BlockSpec(memory_space=pltpu.SMEM)
after = lax.optimization_barrier


def limit(mib):
    return pltpu.CompilerParams(vmem_limit_bytes=mib << 20)


def dot(left, right, dims=NN):
    return lax.dot_general(left, right, dims, preferred_element_type=F32)


def sum_of(terms):
    total = None
    for term in terms:
        total = term if total is None else total + term
    return total


def in_hbm(value):
    return pltpu.with_memory_space_constraint(value, pltpu.HBM)


def local_call(body, outs, operands, scalars=(), cost=None):
    return pl.pallas_call(
        body,
        in_specs=[SCALARS] * len(scalars) + [WIDE] * len(operands),
        out_specs=[WIDE] * len(outs),
        out_shape=[jax.ShapeDtypeStruct(*out) for out in outs],
        compiler_params=limit(8),
        cost_estimate=cost,
    )(*scalars, *operands)


def streamed_call(body, outs, weights, operands, scalars, scratch=()):
    rows, width = weights[0].shape[1:]
    tokens = operands[0].shape[-1]
    cells = sum(w.shape[0] for w in weights)
    return pl.pallas_call(
        body,
        grid=(rows // width,),
        in_specs=[SCALARS] * len(scalars)
        + [pl.BlockSpec((w.shape[0], width, width), lambda n: (0, n, 0)) for w in weights]
        + [WIDE] * len(operands),
        out_specs=[WIDE] * len(outs),
        out_shape=[jax.ShapeDtypeStruct(*out) for out in outs],
        scratch_shapes=list(scratch),
        compiler_params=limit(24),
        cost_estimate=pl.CostEstimate(
            flops=2 * cells * width * rows * tokens,
            bytes_accessed=2 * cells * width * rows,
            transcendentals=0,
        ),
    )(*scalars, *weights, *operands)


def features_first(weights, level, core, pieces):
    _, rows, cells, width = weights.shape
    step, half = 512, cells // 2
    deep = half // max(pieces, 1)

    def body(core_ref, w_ref, o_ref, *s_refs):
        o_ref[...] = jnp.swapaxes(w_ref[0], 0, 1)
        for i, s_ref in enumerate(s_refs):
            s_ref[...] = o_ref[pl.ds(half * core_ref[0] + deep * i, deep)]

    depths = [cells] + [deep] * pieces
    parts = pl.pallas_call(
        body,
        grid_spec=pltpu.PrefetchScalarGridSpec(
            num_scalar_prefetch=1,
            grid=(rows // step,),
            in_specs=[pl.BlockSpec((1, step, cells, width), lambda n, c: (level, n, 0, 0))],
            out_specs=[pl.BlockSpec((k, step, width), lambda n, c: (0, n, 0)) for k in depths],
        ),
        out_shape=[pltpu.HBM((k, rows, width), weights.dtype) for k in depths],
        compiler_params=limit(16),
        cost_estimate=pl.CostEstimate(
            flops=0, bytes_accessed=5 * rows * cells * width, transcendentals=0
        ),
    )(core, weights)
    return in_hbm(parts[0]), [in_hbm(part) for part in parts[1:]]


def in_factor_parts(saved_inputs, proj_in):
    layers, tokens, width = saved_inputs.shape
    rank = proj_in.shape[1]
    half = tokens // 2

    def body(x_ref, p_ref, o_ref):
        for h in range(2):
            part = dot(p_ref[0], x_ref[0, h * half : (h + 1) * half], NT)
            o_ref[h, 0] = part.astype(o_ref.dtype)

    return pl.pallas_call(
        body,
        grid=(layers,),
        in_specs=[
            pl.BlockSpec((1, tokens, width), lambda k: (k, 0, 0)),
            pl.BlockSpec((1, rank, width), lambda k: (k, 0, 0)),
        ],
        out_specs=pl.BlockSpec((2, 1, rank, half), lambda k: (0, k, 0, 0)),
        out_shape=jax.ShapeDtypeStruct((2, layers, rank, half), BF16),
        compiler_params=limit(8),
        cost_estimate=pl.CostEstimate(
            flops=2 * layers * tokens * width * rank,
            bytes_accessed=2 * layers * tokens * width,
            transcendentals=0,
        ),
    )(saved_inputs, proj_in).reshape(2 * layers, rank, half)


def first_partial(gathered, weight, extra):
    cells, tokens, width = gathered.shape
    groups = weight.shape[1] // width
    half = tokens // 2

    def body(w_ref, g_ref, e_ref, o_ref):
        n = pl.program_id(0)
        for h in range(2):
            total = sum_of(
                dot(w_ref[a], g_ref[a, h * half : (h + 1) * half], NT) for a in range(cells)
            )
            o_ref[h * groups + n, :width] = total.astype(o_ref.dtype)

        @pl.when(n == 0)
        def _():
            o_ref[:, width:] = e_ref[...]

    return streamed_call(
        body,
        [((2 * groups, width + extra.shape[1], half), BF16)],
        [weight],
        [gathered, extra],
        [],
    )[0]


def pair_totals(s_ref, g_ref, w_refs):
    own_ref, *others = w_refs
    cells, _, width = own_ref.shape
    half = cells // 2
    deep = others[0].shape[0]
    pieces = half // deep
    x, core = s_ref[0], s_ref[1]
    yield x, sum_of(
        dot(own_ref[a], g_ref[a // 2, (a % 2) * width : (a % 2 + 1) * width]) for a in range(cells)
    )
    yield 1 - x, sum_of(
        dot(
            refs[i // deep][i % deep],
            g_ref[(half // 2) * first + i // 2, (i % 2) * width : (i % 2 + 1) * width],
        )
        for first, refs in ((core, others[:pieces]), (1 - core, others[pieces:]))
        for i in range(half)
    )


def pair_partial(place, gathered, held):
    width = held[0].shape[2]
    groups = held[0].shape[1] // width

    def body(s_ref, *refs):
        *w_refs, g_ref, o_ref = refs
        n = pl.program_id(0)
        for column, total in pair_totals(s_ref, g_ref, w_refs):
            start = pl.multiple_of(column * width, width)
            o_ref[n, pl.ds(start, width)] = total.astype(o_ref.dtype)

        @pl.when(n == 0)
        def _():
            whole = sum_of(g_ref[k, 2 * width :].astype(F32) for k in range(g_ref.shape[0]))
            for k in range(groups):
                o_ref[k, 2 * width :] = whole.astype(o_ref.dtype)

    return streamed_call(
        body, [((groups, *gathered.shape[1:]), BF16)], held, [gathered], [place]
    )[0]


def pair_partial_scored(place, layer_of, gathered, held, outs_top, outs_low, proj, ins):
    width = held[0].shape[2]
    groups = held[0].shape[1] // width
    layers, rank, tokens = ins.shape
    quarter = rank // 4

    def body(s_ref, l_ref, *refs):
        *w_refs, g_ref, a_ref, k_ref, p_ref, i_ref, o_ref, f_ref, last_ref = refs
        n = pl.program_id(0)

        @pl.when(n == 0)
        def _():
            f_ref[3] = a_ref[0]
            f_ref[2] = a_ref[1]
            f_ref[1] = k_ref[0].astype(f_ref.dtype)
            last_ref[...] = k_ref[1]

        for column, total in pair_totals(s_ref, g_ref, w_refs):
            start = pl.multiple_of(column * width, width)
            rounded = total.astype(o_ref.dtype)
            o_ref[n, pl.ds(start, width)] = rounded
            last_ref[...] += dot(p_ref[n, column], rounded)

        @pl.when(n == groups - 1)
        def _():
            f_ref[0] = last_ref[...].astype(f_ref.dtype)
            for o in range(layers):
                block = dot(f_ref[l_ref[o]], i_ref[l_ref[o]], NT).astype(o_ref.dtype)
                o_ref[o, 2 * width :] = jnp.concatenate(
                    [block[quarter * j : quarter * (j + 1)] for j in range(4)], axis=1
                )

    return streamed_call(
        body,
        [((groups, 2 * width + quarter, tokens), BF16)],
        held,
        [gathered, outs_top, outs_low, proj, ins],
        [place, layer_of],
        [pltpu.VMEM((layers, rank, tokens), BF16), pltpu.VMEM((rank, tokens), F32)],
    )[0]


def last_partial(place, gathered, held, kept, extra):
    width = held[0].shape[2]
    groups = held[0].shape[1] // width

    def body(s_ref, *refs):
        *w_refs, g_ref, t_ref, e_ref, o_ref = refs
        n = pl.program_id(0)
        for column, total in pair_totals(s_ref, g_ref, w_refs):
            start = pl.multiple_of(column * width, width)
            mine = t_ref[pl.ds(start, width)]
            total = total + jnp.where(n == s_ref[2], mine, jnp.zeros_like(mine))
            o_ref[groups * column + n, :width] = total.astype(o_ref.dtype)

        @pl.when(n == 0)
        def _():
            for k in range(2 * groups):
                o_ref[k, width:] = e_ref[k % groups]

    return streamed_call(
        body,
        [((2 * groups, width + extra.shape[1], gathered.shape[2]), BF16)],
        held,
        [gathered, kept, extra],
        [place],
    )[0]


def settle_first(place, arrived, gathered, proj_top, proj_next):
    blocks, deep, half = arrived.shape
    width = gathered.shape[2]
    groups = blocks // 2
    rank = proj_top.shape[1]

    def body(s_ref, r_ref, g_ref, p_ref, q_ref, t_ref, c_ref, o_ref):
        x, y = s_ref[0], s_ref[3]
        outs = [None, None]
        for k in range(2):
            start = g_ref[2 * y + k, pl.ds(pl.multiple_of(x * half, half), half)].astype(F32).T
            outs[0] = sum_of([*([outs[0]] if k else []), dot(p_ref[k], start.astype(BF16))])
            total = start + sum_of(r_ref[groups * k + z, :width].astype(F32) for z in range(groups))
            t_ref[k * width : (k + 1) * width] = total
            rounded = total.astype(BF16)
            outs[1] = sum_of([*([outs[1]] if k else []), dot(q_ref[k], rounded)])
            for j in range(c_ref.shape[0]):
                c_ref[j, k * width : (k + 1) * width] = rounded
        ins = sum_of(r_ref[k, width:].astype(F32) for k in range(blocks)).astype(BF16)
        for j in range(c_ref.shape[0]):
            c_ref[j, 2 * width :] = ins
        o_ref[0] = outs[0].astype(BF16)
        o_ref[1] = outs[1].astype(BF16)

    return local_call(
        body,
        [
            ((2 * width, half), F32),
            ((gathered.shape[0] // 2, 2 * width + deep - width, half), BF16),
            ((2, rank, half), BF16),
        ],
        [arrived, gathered, proj_top, proj_next],
        [place],
    )


def settle(arrived, total, proj_next, proj_last):
    groups, deep, half = arrived.shape
    depth = total.shape[0]
    width = depth // 2
    rank = proj_next.shape[1]

    def body(r_ref, t_ref, p_ref, q_ref, o_ref, c_ref, f_ref, i_ref):
        value = t_ref[...] + sum_of(r_ref[z, :depth].astype(F32) for z in range(groups))
        o_ref[...] = value
        rounded = value.astype(BF16)
        for j in range(c_ref.shape[0]):
            c_ref[j] = rounded
        for i, ref in enumerate((p_ref, q_ref)):
            f_ref[i] = dot(ref[0], rounded[:width]) + dot(ref[1], rounded[width:])
        i_ref[...] = r_ref[:, depth:]

    return local_call(
        body,
        [
            (total.shape, F32),
            ((groups, depth, half), BF16),
            ((2, rank, half), F32),
            ((groups, deep - depth, half), BF16),
        ],
        [arrived, total, proj_next, proj_last],
    )


def settle_scored(arrived, total):
    groups, deep, half = arrived.shape
    depth = total.shape[0]

    def body(r_ref, t_ref, o_ref, c_ref):
        value = t_ref[...] + sum_of(r_ref[z, :depth].astype(F32) for z in range(groups))
        o_ref[...] = value
        rounded = value.astype(BF16)
        blocks = sum_of(r_ref[z, depth:].astype(F32) for z in range(groups)).astype(BF16)
        for j in range(c_ref.shape[0]):
            c_ref[j, :depth] = rounded
            c_ref[j, depth:] = blocks

    return local_call(
        body, [(total.shape, F32), ((groups, deep, half), BF16)], [arrived, total]
    )


def finish(place, arrived):
    blocks, _, half = arrived.shape
    groups = blocks // 2
    width = half

    def body(s_ref, r_ref, o_ref, e_ref):
        for k in range(2):
            value = sum_of(r_ref[groups * k + z, :width].astype(F32) for z in range(groups))
            o_ref[k * half : (k + 1) * half] = value.T.astype(o_ref.dtype)
        ends = sum_of(r_ref[groups * s_ref[0] + z, width:].astype(F32) for z in range(groups))
        e_ref[...] = ends[:1, : half // 2] + ends[:1, half // 2 :]

    return local_call(
        body, [((2 * half, width), BF16), ((1, half // 2), F32)], [arrived], [place]
    )


def exchange(blocks, axes, groups=None):
    return lax.all_to_all(blocks, axes, 0, 0, tiled=True, axis_index_groups=groups)


def on_device(saved_inputs, output_grad, weights, proj_in, proj_out, query_grads, owner_map):
    layers, tokens, width = saved_inputs.shape
    rank = proj_in.shape[1]
    rows = weights.shape[1]
    n_dp, n_tensor, n_layer = (lax.axis_size(k) for k in ("dp", "tensor", "layer"))
    n_y = n_tensor // 2
    half = tokens // 2
    t, b = lax.axis_index("tensor"), lax.axis_index("layer")
    x, y = t & 1, t >> 1
    core = lax.axis_index("dp") & 1
    place = jnp.stack([x, core, b, y]).astype(jnp.int32)
    along_y = [[2 * k + j for k in range(n_y)] for j in range(2)]
    along_xz = [[2 * n_layer * k + j for j in range(2 * n_layer)] for k in range(n_y)]
    along_dp_x = [
        [d * n_tensor + 2 * k + j for d in range(n_dp) for j in range(2)] for k in range(n_y)
    ]
    across = [
        (d * n_tensor + k, (d ^ 2) * n_tensor + (k ^ 1)) for d in range(n_dp) for k in range(n_tensor)
    ]
    beside = [(k, k ^ 1) for k in range(n_tensor)]
    flat = pltpu.with_memory_space_constraint(
        weights.reshape(layers, rows, n_tensor, width), pltpu.HBM
    )
    owners = jnp.arange(n_layer, dtype=jnp.int32)
    layer_of = jnp.sum(
        owners[None, :] * (owner_map[None, :] == owners[:, None]).astype(jnp.int32), axis=1
    )

    gathered = exchange(
        jnp.broadcast_to(output_grad, (n_tensor, *output_grad.shape)), "tensor"
    )
    one = core.astype(jnp.int32).reshape(1)
    own, passed, near, far = ([None] * layers for _ in range(4))
    for level, pieces in ((2, 1), (3, 0), (1, 2), (0, 2)):
        own[level], passed[level] = features_first(flat, level, one, pieces)

    def over_both(values):
        return [
            in_hbm(lax.ppermute(values[0], ("dp", "tensor"), across)),
            in_hbm(lax.ppermute(values[1], "tensor", beside)),
        ]

    def to_other_core(values):
        return [in_hbm(lax.ppermute(v, "dp", [(d, d ^ 1) for d in range(n_dp)])) for v in values]

    near[2] = [in_hbm(lax.ppermute(passed[2][0], ("dp", "tensor"), across))]
    other_proj = lax.ppermute(proj_out, "tensor", beside)
    pair_proj = [
        jnp.where(x == 0, jnp.stack([p, q]), jnp.stack([q, p])) for p, q in zip(proj_out, other_proj)
    ]
    shifted = [pair_proj[0]] + [
        lax.ppermute(pair_proj[0], "layer", [(z, z ^ k) for z in range(n_layer)])
        for k in range(1, n_layer)
    ]
    last_proj = jnp.stack(
        [
            sum_of(jnp.where((b ^ k) == z, shifted[k], 0) for k in range(n_layer))
            for z in range(n_layer)
        ]
    ).astype(BF16)
    in_parts = in_factor_parts(saved_inputs, proj_in)
    gathered, own, passed, pair_proj, last_proj, in_parts, place, layer_of = after(
        (gathered, own, passed, pair_proj, last_proj, in_parts, place, layer_of)
    )

    partial = first_partial(gathered, own[3], in_parts)
    arrived = exchange(partial, ("tensor", "layer"), along_xz)
    total, copies, outs_top = settle_first(place, arrived, gathered, pair_proj[3], pair_proj[2])

    passed[1], _ = after((passed[1], total))
    near[1] = over_both(passed[1])
    near[2], _ = after((near[2], total))
    far[2] = to_other_core(near[2])
    gathered = exchange(copies, "tensor", along_y)
    partial = pair_partial(place, gathered, [own[2], *near[2], *far[2]])
    arrived = exchange(partial, "layer")
    total, copies, outs_low, ins = settle(arrived, total, pair_proj[1], pair_proj[0])

    near[1], _ = after((near[1], total))
    far[1] = to_other_core(near[1])
    passed[0], _ = after((passed[0], near[1]))
    near[0] = over_both(passed[0])
    gathered = exchange(copies, "tensor", along_y)
    far[1], gathered = after((far[1], gathered))
    partial = pair_partial_scored(
        place, layer_of, gathered, [own[1], *near[1], *far[1]], outs_top, outs_low, last_proj, ins
    )
    partial, near[0] = after((partial, near[0]))
    far[0] = to_other_core(near[0])
    arrived = exchange(partial, "layer")
    total, copies = settle_scored(arrived, total)

    gathered = exchange(copies, "tensor", along_y)
    summed = gathered[:, 2 * width :].astype(F32).sum(axis=0).astype(BF16)
    every = exchange(
        jnp.broadcast_to(summed, (2 * n_dp, *summed.shape)), ("dp", "tensor"), along_dp_x
    )
    whole = every.reshape(n_dp, 2, rank // 4, 4, rank).astype(F32).sum(axis=1)
    whole = jnp.swapaxes(whole, 1, 2).reshape(n_dp, rank * rank).astype(BF16)
    scored = dot(whole, query_grads[0], NT)
    high = scored.astype(BF16)
    low = (scored - high.astype(F32)).astype(BF16)
    carried = jnp.concatenate([high, low], axis=1)[:, None, :]
    carried = jnp.broadcast_to(carried, (n_dp, 16, carried.shape[2]))
    partial = last_partial(place, gathered, [own[0], *near[0], *far[0]], total, carried)
    arrived = exchange(partial, ("tensor", "layer"), along_xz)
    input_grad, scores = finish(place, arrived)
    return input_grad, scores


def solution(mesh):
    in_specs = (
        P(None, "dp", ("tensor", "layer")),
        P("dp", ("tensor", "layer")),
        P(None, "tensor", None, "layer", None),
        P(None, None, ("tensor", "layer")),
        P(None, None, ("tensor", "layer")),
        P("layer", ("dp", "tensor"), None),
        P(),
    )
    out_specs = (P("dp", ("tensor", "layer")), P("layer", ("dp", "tensor")))
    return jax.shard_map(
        on_device, mesh=mesh, in_specs=in_specs, out_specs=out_specs, check_vma=False
    )
```

```python
import jax
import jax.numpy as jnp
from jax import lax
from jax.experimental import pallas as pl
from jax.experimental.pallas import tpu as pltpu
from jax.sharding import PartitionSpec as P

NT = (((1,), (1,)), ((), ()))
NN = (((1,), (0,)), ((), ()))
F32 = jnp.float32
BF16 = jnp.bfloat16
WIDE = pl.BlockSpec(memory_space=pltpu.VMEM)
SCALARS = pl.BlockSpec(memory_space=pltpu.SMEM)
after = lax.optimization_barrier


def limit(mib):
    return pltpu.CompilerParams(vmem_limit_bytes=mib << 20)


def dot(left, right, dims=NN):
    return lax.dot_general(left, right, dims, preferred_element_type=F32)


def sum_of(terms):
    total = None
    for term in terms:
        total = term if total is None else total + term
    return total


def in_hbm(value):
    return pltpu.with_memory_space_constraint(value, pltpu.HBM)


def local_call(body, outs, operands, scalars=(), cost=None):
    return pl.pallas_call(
        body,
        in_specs=[SCALARS] * len(scalars) + [WIDE] * len(operands),
        out_specs=[WIDE] * len(outs),
        out_shape=[jax.ShapeDtypeStruct(*out) for out in outs],
        compiler_params=limit(8),
        cost_estimate=cost,
    )(*scalars, *operands)


def streamed_call(body, outs, weights, operands, scalars, scratch=()):
    rows, width = weights[0].shape[1:]
    tokens = operands[0].shape[-1]
    cells = sum(w.shape[0] for w in weights)
    groups = rows // width
    sizes = [len(scalars), len(weights), len(operands), len(outs), len(weights), len(scratch)]

    def kernel(*refs):
        parts, at = [], 0
        for size in sizes:
            parts.append(refs[at : at + size])
            at += size
        scalar_refs, far_refs, operand_refs, out_refs, held_refs, scratch_refs = parts
        sems = refs[-1]

        def copy(k, n):
            rows_of = pl.ds(n * width, width)
            return pltpu.make_async_copy(
                far_refs[k].at[:, rows_of], held_refs[k].at[:, rows_of], sems.at[k, n]
            )

        for n in range(groups):
            for k in range(len(weights)):
                copy(k, n).start()

        def fetch(n):
            for k in range(len(weights)):
                copy(k, n).wait()

        body(fetch, scalar_refs, held_refs, operand_refs, out_refs, scratch_refs)

    return pl.pallas_call(
        kernel,
        in_specs=[SCALARS] * len(scalars)
        + [pl.BlockSpec(memory_space=pltpu.HBM)] * len(weights)
        + [WIDE] * len(operands),
        out_specs=[WIDE] * len(outs),
        out_shape=[jax.ShapeDtypeStruct(*out) for out in outs],
        scratch_shapes=[pltpu.VMEM(w.shape, w.dtype) for w in weights]
        + list(scratch)
        + [pltpu.SemaphoreType.DMA((len(weights), groups))],
        compiler_params=limit(20),
        cost_estimate=pl.CostEstimate(
            flops=2 * cells * width * rows * tokens,
            bytes_accessed=2 * cells * width * rows,
            transcendentals=0,
        ),
    )(*scalars, *weights, *operands)


def features_first(weights, level, core, pieces):
    _, rows, cells, width = weights.shape
    step, half = 512, cells // 2
    deep = half // max(pieces, 1)

    def body(core_ref, w_ref, o_ref, *s_refs):
        o_ref[...] = jnp.swapaxes(w_ref[0], 0, 1)
        for i, s_ref in enumerate(s_refs):
            s_ref[...] = o_ref[pl.ds(half * core_ref[0] + deep * i, deep)]

    depths = [cells] + [deep] * pieces
    parts = pl.pallas_call(
        body,
        grid_spec=pltpu.PrefetchScalarGridSpec(
            num_scalar_prefetch=1,
            grid=(rows // step,),
            in_specs=[pl.BlockSpec((1, step, cells, width), lambda n, c: (level, n, 0, 0))],
            out_specs=[pl.BlockSpec((k, step, width), lambda n, c: (0, n, 0)) for k in depths],
        ),
        out_shape=[pltpu.HBM((k, rows, width), weights.dtype) for k in depths],
        compiler_params=limit(16),
        cost_estimate=pl.CostEstimate(
            flops=0, bytes_accessed=5 * rows * cells * width, transcendentals=0
        ),
    )(core, weights)
    return in_hbm(parts[0]), [in_hbm(part) for part in parts[1:]]


def in_factor_parts(saved_inputs, proj_in):
    layers, tokens, width = saved_inputs.shape
    rank = proj_in.shape[1]
    half = tokens // 2

    def body(x_ref, p_ref, o_ref):
        for h in range(2):
            part = dot(p_ref[0], x_ref[0, h * half : (h + 1) * half], NT)
            o_ref[h, 0] = part.astype(o_ref.dtype)

    return pl.pallas_call(
        body,
        grid=(layers,),
        in_specs=[
            pl.BlockSpec((1, tokens, width), lambda k: (k, 0, 0)),
            pl.BlockSpec((1, rank, width), lambda k: (k, 0, 0)),
        ],
        out_specs=pl.BlockSpec((2, 1, rank, half), lambda k: (0, k, 0, 0)),
        out_shape=jax.ShapeDtypeStruct((2, layers, rank, half), BF16),
        compiler_params=limit(8),
        cost_estimate=pl.CostEstimate(
            flops=2 * layers * tokens * width * rank,
            bytes_accessed=2 * layers * tokens * width,
            transcendentals=0,
        ),
    )(saved_inputs, proj_in).reshape(2 * layers, rank, half)


def first_partial(gathered, weight, extra):
    cells, tokens, width = gathered.shape
    groups = weight.shape[1] // width
    half = tokens // 2

    def body(fetch, _, weight_refs, operand_refs, out_refs, __):
        (w_ref,), (g_ref, e_ref), (o_ref,) = weight_refs, operand_refs, out_refs
        o_ref[:, width:] = e_ref[...]
        for n in range(groups):
            fetch(n)
            for h in range(2):
                total = sum_of(
                    dot(
                        w_ref[a, n * width : (n + 1) * width],
                        g_ref[a, h * half : (h + 1) * half],
                        NT,
                    )
                    for a in range(cells)
                )
                o_ref[h * groups + n, :width] = total.astype(o_ref.dtype)

    return streamed_call(
        body,
        [((2 * groups, width + extra.shape[1], half), BF16)],
        [weight],
        [gathered, extra],
        [],
    )[0]


def pair_totals(s_ref, g_ref, w_refs, n):
    own_ref, *others = w_refs
    cells, _, width = own_ref.shape
    half = cells // 2
    deep = others[0].shape[0]
    pieces = half // deep
    x, core = s_ref[0], s_ref[1]
    cut = slice(n * width, (n + 1) * width)
    yield x, sum_of(
        dot(own_ref[a, cut], g_ref[a // 2, (a % 2) * width : (a % 2 + 1) * width])
        for a in range(cells)
    )
    yield 1 - x, sum_of(
        dot(
            refs[i // deep][i % deep, cut],
            g_ref[(half // 2) * first + i // 2, (i % 2) * width : (i % 2 + 1) * width],
        )
        for first, refs in ((core, others[:pieces]), (1 - core, others[pieces:]))
        for i in range(half)
    )


def pair_partial(place, gathered, held):
    width = held[0].shape[2]
    groups = held[0].shape[1] // width

    def body(fetch, scalar_refs, w_refs, operand_refs, out_refs, _):
        (s_ref,), (g_ref,), (o_ref,) = scalar_refs, operand_refs, out_refs
        whole = sum_of(g_ref[k, 2 * width :].astype(F32) for k in range(g_ref.shape[0]))
        for n in range(groups):
            o_ref[n, 2 * width :] = whole.astype(o_ref.dtype)
            fetch(n)
            for column, total in pair_totals(s_ref, g_ref, w_refs, n):
                start = pl.multiple_of(column * width, width)
                o_ref[n, pl.ds(start, width)] = total.astype(o_ref.dtype)

    return streamed_call(
        body, [((groups, *gathered.shape[1:]), BF16)], held, [gathered], [place]
    )[0]


def pair_partial_scored(place, layer_of, gathered, held, grads, proj, last_proj, ins):
    width = held[0].shape[2]
    groups = held[0].shape[1] // width
    layers, rank, tokens = ins.shape
    quarter = rank // 4

    def body(fetch, scalar_refs, w_refs, operand_refs, out_refs, scratch_refs):
        s_ref, l_ref = scalar_refs
        g_ref, *grad_refs, p_ref, q_ref, i_ref = operand_refs
        (o_ref,), (f_ref,) = out_refs, scratch_refs

        def factor(level, ref):
            return dot(p_ref[level, 0], ref[:width]) + dot(p_ref[level, 1], ref[width : 2 * width])

        for k, ref in enumerate(grad_refs):
            f_ref[layers - 1 - k] = factor(layers - 1 - k, ref).astype(f_ref.dtype)
        final = factor(0, grad_refs[-1])
        for n in range(groups):
            fetch(n)
            for column, total in pair_totals(s_ref, g_ref, w_refs, n):
                start = pl.multiple_of(column * width, width)
                rounded = total.astype(o_ref.dtype)
                o_ref[n, pl.ds(start, width)] = rounded
                final = final + dot(q_ref[n, column], rounded)
        f_ref[0] = final.astype(f_ref.dtype)
        for o in range(layers):
            block = dot(f_ref[l_ref[o]], i_ref[l_ref[o]], NT).astype(o_ref.dtype)
            o_ref[o, 2 * width :] = jnp.concatenate(
                [block[quarter * j : quarter * (j + 1)] for j in range(4)], axis=1
            )

    return streamed_call(
        body,
        [((groups, 2 * width + quarter, tokens), BF16)],
        held,
        [gathered, *grads, proj, last_proj, ins],
        [place, layer_of],
        [pltpu.VMEM((layers, rank, tokens), BF16)],
    )[0]


def last_partial(place, gathered, held, kept, extra):
    width = held[0].shape[2]
    groups = held[0].shape[1] // width

    def body(fetch, scalar_refs, w_refs, operand_refs, out_refs, _):
        (s_ref,), (g_ref, t_ref, e_ref), (o_ref,) = scalar_refs, operand_refs, out_refs
        for k in range(2 * groups):
            o_ref[k, width:] = e_ref[k % groups]
        for n in range(groups):
            fetch(n)
            for column, total in pair_totals(s_ref, g_ref, w_refs, n):
                start = pl.multiple_of(column * width, width)
                mine = t_ref[pl.ds(start, width)]
                total = total + jnp.where(n == s_ref[2], mine, jnp.zeros_like(mine))
                o_ref[groups * column + n, :width] = total.astype(o_ref.dtype)

    return streamed_call(
        body,
        [((2 * groups, width + extra.shape[1], gathered.shape[2]), BF16)],
        held,
        [gathered, kept, extra],
        [place],
    )[0]


def settle_first(place, arrived, gathered):
    blocks, deep, half = arrived.shape
    width = gathered.shape[2]
    groups = blocks // 2

    def body(s_ref, r_ref, g_ref, t_ref, c_ref, b_ref, m_ref):
        x, y = s_ref[0], s_ref[3]
        for k in range(2):
            rows_of = slice(k * width, (k + 1) * width)
            start = g_ref[2 * y + k, pl.ds(pl.multiple_of(x * half, half), half)].astype(F32).T
            b_ref[rows_of] = start.astype(BF16)
            total = start + sum_of(r_ref[groups * k + z, :width].astype(F32) for z in range(groups))
            t_ref[rows_of] = total
            rounded = total.astype(BF16)
            m_ref[rows_of] = rounded
            for j in range(c_ref.shape[0]):
                c_ref[j, rows_of] = rounded
        ins = sum_of(r_ref[k, width:].astype(F32) for k in range(blocks)).astype(BF16)
        for j in range(c_ref.shape[0]):
            c_ref[j, 2 * width :] = ins

    return local_call(
        body,
        [
            ((2 * width, half), F32),
            ((gathered.shape[0] // 2, 2 * width + deep - width, half), BF16),
            ((2 * width, half), BF16),
            ((2 * width, half), BF16),
        ],
        [arrived, gathered],
        [place],
    )


def settle(arrived, total):
    groups, deep, half = arrived.shape
    depth = total.shape[0]

    def body(r_ref, t_ref, o_ref, c_ref, m_ref, i_ref):
        value = t_ref[...] + sum_of(r_ref[z, :depth].astype(F32) for z in range(groups))
        o_ref[...] = value
        rounded = value.astype(BF16)
        m_ref[...] = rounded
        for j in range(c_ref.shape[0]):
            c_ref[j] = rounded
        i_ref[...] = r_ref[:, depth:]

    return local_call(
        body,
        [
            (total.shape, F32),
            ((groups, depth, half), BF16),
            (total.shape, BF16),
            ((groups, deep - depth, half), BF16),
        ],
        [arrived, total],
    )


def settle_scored(arrived, total):
    groups, deep, half = arrived.shape
    depth = total.shape[0]

    def body(r_ref, t_ref, o_ref, c_ref):
        value = t_ref[...] + sum_of(r_ref[z, :depth].astype(F32) for z in range(groups))
        o_ref[...] = value
        rounded = value.astype(BF16)
        blocks = sum_of(r_ref[z, depth:].astype(F32) for z in range(groups)).astype(BF16)
        for j in range(c_ref.shape[0]):
            c_ref[j, :depth] = rounded
            c_ref[j, depth:] = blocks

    return local_call(
        body, [(total.shape, F32), ((groups, deep, half), BF16)], [arrived, total]
    )


def finish(place, arrived):
    blocks, _, half = arrived.shape
    groups = blocks // 2
    width = half

    def body(s_ref, r_ref, o_ref, e_ref):
        for k in range(2):
            value = sum_of(r_ref[groups * k + z, :width].astype(F32) for z in range(groups))
            o_ref[k * half : (k + 1) * half] = value.T.astype(o_ref.dtype)
        ends = sum_of(r_ref[groups * s_ref[0] + z, width:].astype(F32) for z in range(groups))
        e_ref[...] = ends[:1, : half // 2] + ends[:1, half // 2 :]

    return local_call(
        body, [((2 * half, width), BF16), ((1, half // 2), F32)], [arrived], [place]
    )


def exchange(blocks, axes, groups=None):
    return lax.all_to_all(blocks, axes, 0, 0, tiled=True, axis_index_groups=groups)


def on_device(saved_inputs, output_grad, weights, proj_in, proj_out, query_grads, owner_map):
    layers, tokens, width = saved_inputs.shape
    rank = proj_in.shape[1]
    rows = weights.shape[1]
    n_dp, n_tensor, n_layer = (lax.axis_size(k) for k in ("dp", "tensor", "layer"))
    n_y = n_tensor // 2
    half = tokens // 2
    t, b = lax.axis_index("tensor"), lax.axis_index("layer")
    x, y = t & 1, t >> 1
    core = lax.axis_index("dp") & 1
    place = jnp.stack([x, core, b, y]).astype(jnp.int32)
    along_y = [[2 * k + j for k in range(n_y)] for j in range(2)]
    along_xz = [[2 * n_layer * k + j for j in range(2 * n_layer)] for k in range(n_y)]
    along_dp_x = [
        [d * n_tensor + 2 * k + j for d in range(n_dp) for j in range(2)] for k in range(n_y)
    ]
    across = [
        (d * n_tensor + k, (d ^ 2) * n_tensor + (k ^ 1)) for d in range(n_dp) for k in range(n_tensor)
    ]
    beside = [(k, k ^ 1) for k in range(n_tensor)]
    flat = pltpu.with_memory_space_constraint(
        weights.reshape(layers, rows, n_tensor, width), pltpu.HBM
    )
    owners = jnp.arange(n_layer, dtype=jnp.int32)
    layer_of = jnp.sum(
        owners[None, :] * (owner_map[None, :] == owners[:, None]).astype(jnp.int32), axis=1
    )

    gathered = exchange(
        jnp.broadcast_to(output_grad, (n_tensor, *output_grad.shape)), "tensor"
    )
    one = core.astype(jnp.int32).reshape(1)
    own, passed, near, far = ([None] * layers for _ in range(4))
    for level, pieces in ((2, 1), (3, 0), (1, 2), (0, 2)):
        own[level], passed[level] = features_first(flat, level, one, pieces)

    def over_both(values):
        return [
            in_hbm(lax.ppermute(values[0], ("dp", "tensor"), across)),
            in_hbm(lax.ppermute(values[1], "tensor", beside)),
        ]

    def to_other_core(values):
        return [in_hbm(lax.ppermute(v, "dp", [(d, d ^ 1) for d in range(n_dp)])) for v in values]

    near[2] = [in_hbm(lax.ppermute(passed[2][0], ("dp", "tensor"), across))]
    in_parts = in_factor_parts(saved_inputs, proj_in)
    gathered, own[3], own[2], own[1], passed[1], in_parts, place, layer_of = after(
        (gathered, own[3], own[2], own[1], passed[1], in_parts, place, layer_of)
    )

    partial = first_partial(gathered, own[3], in_parts)
    arrived = exchange(partial, ("tensor", "layer"), along_xz)
    total, copies, above_3, above_2 = settle_first(place, arrived, gathered)

    passed[1], proj_out, _ = after((passed[1], proj_out, total))
    other_proj = lax.ppermute(proj_out, "tensor", beside)
    pair_proj = jnp.where(
        x == 0, jnp.stack([proj_out, other_proj], 1), jnp.stack([other_proj, proj_out], 1)
    )
    shifted = [pair_proj[0]] + [
        lax.ppermute(pair_proj[0], "layer", [(z, z ^ k) for z in range(n_layer)])
        for k in range(1, n_layer)
    ]
    last_proj = jnp.stack(
        [
            sum_of(jnp.where((b ^ k) == z, shifted[k], 0) for k in range(n_layer))
            for z in range(n_layer)
        ]
    ).astype(BF16)
    near[1] = over_both(passed[1])
    near[2], _ = after((near[2], total))
    far[2] = to_other_core(near[2])
    gathered = exchange(copies, "tensor", along_y)
    gathered, own[0], passed[0], pair_proj, last_proj = after(
        (gathered, own[0], passed[0], pair_proj, last_proj)
    )
    partial = pair_partial(place, gathered, [own[2], *near[2], *far[2]])
    arrived = exchange(partial, "layer")
    total, copies, above_1, ins = settle(arrived, total)

    near[1], _ = after((near[1], total))
    far[1] = to_other_core(near[1])
    passed[0], _ = after((passed[0], near[1]))
    near[0] = over_both(passed[0])
    gathered = exchange(copies, "tensor", along_y)
    far[1], gathered = after((far[1], gathered))
    partial = pair_partial_scored(
        place,
        layer_of,
        gathered,
        [own[1], *near[1], *far[1]],
        [above_3, above_2, above_1],
        pair_proj,
        last_proj,
        ins,
    )
    partial, near[0] = after((partial, near[0]))
    far[0] = to_other_core(near[0])
    arrived = exchange(partial, "layer")
    arrived, far[0] = after((arrived, far[0]))
    total, copies = settle_scored(arrived, total)

    gathered = exchange(copies, "tensor", along_y)
    summed = gathered[:, 2 * width :].astype(F32).sum(axis=0).astype(BF16)
    every = exchange(
        jnp.broadcast_to(summed, (2 * n_dp, *summed.shape)), ("dp", "tensor"), along_dp_x
    )
    whole = every.reshape(n_dp, 2, rank // 4, 4, rank).astype(F32).sum(axis=1)
    whole = jnp.swapaxes(whole, 1, 2).reshape(n_dp, rank * rank).astype(BF16)
    scored = dot(whole, query_grads[0], NT)
    high = scored.astype(BF16)
    low = (scored - high.astype(F32)).astype(BF16)
    carried = jnp.concatenate([high, low], axis=1)[:, None, :]
    carried = jnp.broadcast_to(carried, (n_dp, 16, carried.shape[2]))
    partial = last_partial(place, gathered, [own[0], *near[0], *far[0]], total, carried)
    arrived = exchange(partial, ("tensor", "layer"), along_xz)
    input_grad, scores = finish(place, arrived)
    return input_grad, scores


def solution(mesh):
    in_specs = (
        P(None, "dp", ("tensor", "layer")),
        P("dp", ("tensor", "layer")),
        P(None, "tensor", None, "layer", None),
        P(None, None, ("tensor", "layer")),
        P(None, None, ("tensor", "layer")),
        P("layer", ("dp", "tensor"), None),
        P(),
    )
    out_specs = (P("dp", ("tensor", "layer")), P("layer", ("dp", "tensor")))
    return jax.shard_map(
        on_device, mesh=mesh, in_specs=in_specs, out_specs=out_specs, check_vma=False
    )
```

```python
import jax
import jax.numpy as jnp
from jax import lax
from jax.experimental import pallas as pl
from jax.experimental.pallas import tpu as pltpu
from jax.sharding import PartitionSpec as P

NT = (((1,), (1,)), ((), ()))
NN = (((1,), (0,)), ((), ()))
F32 = jnp.float32
BF16 = jnp.bfloat16
WIDE = pl.BlockSpec(memory_space=pltpu.VMEM)
SCALARS = pl.BlockSpec(memory_space=pltpu.SMEM)
after = lax.optimization_barrier


def limit(mib):
    return pltpu.CompilerParams(vmem_limit_bytes=mib << 20)


def dot(left, right, dims=NN):
    return lax.dot_general(left, right, dims, preferred_element_type=F32)


def sum_of(terms):
    total = None
    for term in terms:
        total = term if total is None else total + term
    return total


def in_hbm(value):
    return pltpu.with_memory_space_constraint(value, pltpu.HBM)


def local_call(body, outs, operands, scalars=(), cost=None, to_hbm=()):
    def whole(out):
        return pl.BlockSpec(out[0], lambda: (0,) * len(out[0]))

    return pl.pallas_call(
        body,
        in_specs=[SCALARS] * len(scalars) + [WIDE] * len(operands),
        out_specs=[whole(out) if i in to_hbm else WIDE for i, out in enumerate(outs)],
        out_shape=[
            pltpu.HBM(*out) if i in to_hbm else jax.ShapeDtypeStruct(*out)
            for i, out in enumerate(outs)
        ],
        compiler_params=limit(8),
        cost_estimate=cost,
    )(*scalars, *operands)


def streamed_call(body, outs, weights, operands, scalars, scratch=(), late=()):
    rows, width = weights[0].shape[1:]
    tokens = operands[0].shape[-1]
    cells = sum(w.shape[0] for w in weights)
    groups = rows // width
    moved = [*weights, *late]
    sizes = [
        len(scalars), len(moved), len(operands), len(outs), len(moved), len(scratch),
    ]

    def kernel(*refs):
        parts, at = [], 0
        for size in sizes:
            parts.append(refs[at : at + size])
            at += size
        scalar_refs, far_refs, operand_refs, out_refs, held_refs, scratch_refs = parts
        sems = refs[-1]
        count = len(weights)

        def copies(n):
            if n < 0:
                return [
                    pltpu.make_async_copy(far_refs[k], held_refs[k], sems.at[k, 0])
                    for k in range(count, len(moved))
                ]
            rows_of = pl.ds(n * width, width)
            return [
                pltpu.make_async_copy(
                    far_refs[k].at[:, rows_of], held_refs[k].at[:, rows_of], sems.at[k, n]
                )
                for k in range(count)
            ]

        for n in [*range(groups), -1]:
            for copy in copies(n):
                copy.start()

        def fetch(n):
            for copy in copies(n):
                copy.wait()

        body(
            fetch,
            scalar_refs,
            held_refs[:count],
            [*operand_refs, *held_refs[count:]],
            out_refs,
            scratch_refs,
        )

    return pl.pallas_call(
        kernel,
        in_specs=[SCALARS] * len(scalars)
        + [pl.BlockSpec(memory_space=pltpu.HBM)] * len(moved)
        + [WIDE] * len(operands),
        out_specs=[WIDE] * len(outs),
        out_shape=[jax.ShapeDtypeStruct(*out) for out in outs],
        scratch_shapes=[pltpu.VMEM(w.shape, w.dtype) for w in moved]
        + list(scratch)
        + [pltpu.SemaphoreType.DMA((len(moved), groups))],
        compiler_params=limit(20),
        cost_estimate=pl.CostEstimate(
            flops=2 * cells * width * rows * tokens,
            bytes_accessed=2 * cells * width * rows,
            transcendentals=0,
        ),
    )(*scalars, *moved, *operands)


def features_first(weights, level, core, pieces):
    _, rows, cells, width = weights.shape
    step, half = 512, cells // 2
    deep = half // max(pieces, 1)

    def body(core_ref, w_ref, o_ref, *s_refs):
        o_ref[...] = jnp.swapaxes(w_ref[0], 0, 1)
        for i, s_ref in enumerate(s_refs):
            s_ref[...] = o_ref[pl.ds(half * core_ref[0] + deep * i, deep)]

    depths = [cells] + [deep] * pieces
    parts = pl.pallas_call(
        body,
        grid_spec=pltpu.PrefetchScalarGridSpec(
            num_scalar_prefetch=1,
            grid=(rows // step,),
            in_specs=[pl.BlockSpec((1, step, cells, width), lambda n, c: (level, n, 0, 0))],
            out_specs=[pl.BlockSpec((k, step, width), lambda n, c: (0, n, 0)) for k in depths],
        ),
        out_shape=[pltpu.HBM((k, rows, width), weights.dtype) for k in depths],
        compiler_params=limit(16),
        cost_estimate=pl.CostEstimate(
            flops=0, bytes_accessed=5 * rows * cells * width, transcendentals=0
        ),
    )(core, weights)
    return in_hbm(parts[0]), [in_hbm(part) for part in parts[1:]]


def in_factor_parts(saved_inputs, proj_in):
    layers, tokens, width = saved_inputs.shape
    rank = proj_in.shape[1]
    half = tokens // 2

    def body(x_ref, p_ref, o_ref):
        for h in range(2):
            part = dot(p_ref[0], x_ref[0, h * half : (h + 1) * half], NT)
            o_ref[h, 0] = part.astype(o_ref.dtype)

    return pl.pallas_call(
        body,
        grid=(layers,),
        in_specs=[
            pl.BlockSpec((1, tokens, width), lambda k: (k, 0, 0)),
            pl.BlockSpec((1, rank, width), lambda k: (k, 0, 0)),
        ],
        out_specs=pl.BlockSpec((2, 1, rank, half), lambda k: (0, k, 0, 0)),
        out_shape=jax.ShapeDtypeStruct((2, layers, rank, half), BF16),
        compiler_params=limit(8),
        cost_estimate=pl.CostEstimate(
            flops=2 * layers * tokens * width * rank,
            bytes_accessed=2 * layers * tokens * width,
            transcendentals=0,
        ),
    )(saved_inputs, proj_in).reshape(2 * layers, rank, half)


def first_partial(gathered, weight, extra):
    cells, tokens, width = gathered.shape
    groups = weight.shape[1] // width
    half = tokens // 2

    def body(fetch, _, weight_refs, operand_refs, out_refs, __):
        (w_ref,), (g_ref, e_ref), (o_ref,) = weight_refs, operand_refs, out_refs
        o_ref[:, width:] = e_ref[...]
        for n in range(groups):
            fetch(n)
            for h in range(2):
                total = sum_of(
                    dot(
                        w_ref[a, n * width : (n + 1) * width],
                        g_ref[a, h * half : (h + 1) * half],
                        NT,
                    )
                    for a in range(cells)
                )
                o_ref[h * groups + n, :width] = total.astype(o_ref.dtype)

    return streamed_call(
        body,
        [((2 * groups, width + extra.shape[1], half), BF16)],
        [weight],
        [gathered, extra],
        [],
    )[0]


def pair_totals(s_ref, g_ref, w_refs, n):
    own_ref, *others = w_refs
    cells, _, width = own_ref.shape
    half = cells // 2
    deep = others[0].shape[0]
    pieces = half // deep
    x, core = s_ref[0], s_ref[1]
    cut = slice(n * width, (n + 1) * width)
    yield x, sum_of(
        dot(own_ref[a, cut], g_ref[a // 2, (a % 2) * width : (a % 2 + 1) * width])
        for a in range(cells)
    )
    yield 1 - x, sum_of(
        dot(
            refs[i // deep][i % deep, cut],
            g_ref[(half // 2) * first + i // 2, (i % 2) * width : (i % 2 + 1) * width],
        )
        for first, refs in ((core, others[:pieces]), (1 - core, others[pieces:]))
        for i in range(half)
    )


def pair_partial(place, gathered, held):
    width = held[0].shape[2]
    groups = held[0].shape[1] // width

    def body(fetch, scalar_refs, w_refs, operand_refs, out_refs, _):
        (s_ref,), (g_ref,), (o_ref,) = scalar_refs, operand_refs, out_refs
        whole = sum_of(g_ref[k, 2 * width :].astype(F32) for k in range(g_ref.shape[0]))
        for n in range(groups):
            o_ref[n, 2 * width :] = whole.astype(o_ref.dtype)
            fetch(n)
            for column, total in pair_totals(s_ref, g_ref, w_refs, n):
                start = pl.multiple_of(column * width, width)
                o_ref[n, pl.ds(start, width)] = total.astype(o_ref.dtype)

    return streamed_call(
        body, [((groups, *gathered.shape[1:]), BF16)], held, [gathered], [place]
    )[0]


def pair_partial_scored(place, layer_of, gathered, held, grads, proj, last_proj, ins):
    width = held[0].shape[2]
    groups = held[0].shape[1] // width
    layers, rank, tokens = ins.shape
    quarter = rank // 4

    def body(fetch, scalar_refs, w_refs, operand_refs, out_refs, scratch_refs):
        s_ref, l_ref = scalar_refs
        g_ref, *grad_refs, p_ref, q_ref, i_ref = operand_refs
        (o_ref,), (f_ref,) = out_refs, scratch_refs

        def factor(level, ref):
            return dot(p_ref[level, 0], ref[:width]) + dot(p_ref[level, 1], ref[width : 2 * width])

        for k, ref in enumerate(grad_refs):
            f_ref[layers - 1 - k] = factor(layers - 1 - k, ref).astype(f_ref.dtype)
        final = factor(0, grad_refs[-1])
        for n in range(groups):
            fetch(n)
            for column, total in pair_totals(s_ref, g_ref, w_refs, n):
                start = pl.multiple_of(column * width, width)
                rounded = total.astype(o_ref.dtype)
                o_ref[n, pl.ds(start, width)] = rounded
                final = final + dot(q_ref[n, column], rounded)
        f_ref[0] = final.astype(f_ref.dtype)
        for o in range(layers):
            block = dot(f_ref[l_ref[o]], i_ref[l_ref[o]], NT).astype(o_ref.dtype)
            o_ref[o, 2 * width :] = jnp.concatenate(
                [block[quarter * j : quarter * (j + 1)] for j in range(4)], axis=1
            )

    return streamed_call(
        body,
        [((groups, 2 * width + quarter, tokens), BF16)],
        held,
        [gathered, *grads, proj, last_proj, ins],
        [place, layer_of],
        [pltpu.VMEM((layers, rank, tokens), BF16)],
    )[0]


def last_partial(place, gathered, held, kept, under):
    width = held[0].shape[2]
    groups = held[0].shape[1] // width

    def body(fetch, scalar_refs, w_refs, operand_refs, out_refs, _):
        (s_ref,), (g_ref, t_ref), (o_ref,) = scalar_refs, operand_refs, out_refs
        for k in range(2 * groups):
            o_ref[k, width:] = jnp.zeros((under, o_ref.shape[2]), o_ref.dtype)
        fetch(-1)
        for n in range(groups):
            fetch(n)
            for column, total in pair_totals(s_ref, g_ref, w_refs, n):
                start = pl.multiple_of(column * width, width)
                mine = t_ref[pl.ds(start, width)]
                total = total + jnp.where(n == s_ref[2], mine, jnp.zeros_like(mine))
                o_ref[groups * column + n, :width] = total.astype(o_ref.dtype)

    return streamed_call(
        body,
        [((2 * groups, width + under, gathered.shape[2]), BF16)],
        held,
        [gathered],
        [place],
        late=[kept],
    )[0]


def put_under(partial, extra):
    blocks, deep, _ = partial.shape
    groups, rows, _ = extra.shape

    def body(_, e_ref, o_ref, sems):
        copies = [
            pltpu.make_async_copy(
                e_ref.at[k % groups], o_ref.at[k, pl.ds(deep - rows, rows)], sems.at[k]
            )
            for k in range(blocks)
        ]
        for copy in copies:
            copy.start()
        for copy in copies:
            copy.wait()

    return pl.pallas_call(
        body,
        in_specs=[pl.BlockSpec(memory_space=pl.ANY), WIDE],
        out_specs=pl.BlockSpec(memory_space=pl.ANY),
        out_shape=jax.ShapeDtypeStruct(partial.shape, partial.dtype),
        scratch_shapes=[pltpu.SemaphoreType.DMA((blocks,))],
        input_output_aliases={0: 0},
        compiler_params=limit(4),
    )(partial, extra)


def settle_first(place, arrived, gathered):
    blocks, deep, half = arrived.shape
    width = gathered.shape[2]
    groups = blocks // 2

    def body(s_ref, r_ref, g_ref, t_ref, c_ref, b_ref, m_ref):
        x, y = s_ref[0], s_ref[3]
        for k in range(2):
            rows_of = slice(k * width, (k + 1) * width)
            start = g_ref[2 * y + k, pl.ds(pl.multiple_of(x * half, half), half)].astype(F32).T
            b_ref[rows_of] = start.astype(BF16)
            total = start + sum_of(r_ref[groups * k + z, :width].astype(F32) for z in range(groups))
            t_ref[rows_of] = total
            rounded = total.astype(BF16)
            m_ref[rows_of] = rounded
            for j in range(c_ref.shape[0]):
                c_ref[j, rows_of] = rounded
        ins = sum_of(r_ref[k, width:].astype(F32) for k in range(blocks)).astype(BF16)
        for j in range(c_ref.shape[0]):
            c_ref[j, 2 * width :] = ins

    return local_call(
        body,
        [
            ((2 * width, half), F32),
            ((gathered.shape[0] // 2, 2 * width + deep - width, half), BF16),
            ((2 * width, half), BF16),
            ((2 * width, half), BF16),
        ],
        [arrived, gathered],
        [place],
        to_hbm=(0, 1, 2, 3),
    )


def settle(arrived, total):
    groups, deep, half = arrived.shape
    depth = total.shape[0]

    def body(r_ref, t_ref, o_ref, c_ref, m_ref, i_ref):
        value = t_ref[...] + sum_of(r_ref[z, :depth].astype(F32) for z in range(groups))
        o_ref[...] = value
        rounded = value.astype(BF16)
        m_ref[...] = rounded
        for j in range(c_ref.shape[0]):
            c_ref[j] = rounded
        i_ref[...] = r_ref[:, depth:]

    return local_call(
        body,
        [
            (total.shape, F32),
            ((groups, depth, half), BF16),
            (total.shape, BF16),
            ((groups, deep - depth, half), BF16),
        ],
        [arrived, total],
    )


def settle_scored(arrived, total):
    groups, deep, half = arrived.shape
    depth = total.shape[0]

    def body(r_ref, t_ref, o_ref, c_ref):
        value = t_ref[...] + sum_of(r_ref[z, :depth].astype(F32) for z in range(groups))
        o_ref[...] = value
        rounded = value.astype(BF16)
        blocks = sum_of(r_ref[z, depth:].astype(F32) for z in range(groups)).astype(BF16)
        for j in range(c_ref.shape[0]):
            c_ref[j, :depth] = rounded
            c_ref[j, depth:] = blocks

    return local_call(
        body,
        [(total.shape, F32), ((groups, deep, half), BF16)],
        [arrived, total],
        to_hbm=(0,),
    )


def finish(place, arrived):
    blocks, _, half = arrived.shape
    groups = blocks // 2
    width = half

    def body(s_ref, r_ref, o_ref, e_ref):
        for k in range(2):
            value = sum_of(r_ref[groups * k + z, :width].astype(F32) for z in range(groups))
            o_ref[k * half : (k + 1) * half] = value.T.astype(o_ref.dtype)
        ends = sum_of(r_ref[groups * s_ref[0] + z, width:].astype(F32) for z in range(groups))
        e_ref[...] = ends[:1, : half // 2] + ends[:1, half // 2 :]

    return local_call(
        body, [((2 * half, width), BF16), ((1, half // 2), F32)], [arrived], [place]
    )


def exchange(blocks, axes, groups=None):
    return lax.all_to_all(blocks, axes, 0, 0, tiled=True, axis_index_groups=groups)


def on_device(saved_inputs, output_grad, weights, proj_in, proj_out, query_grads, owner_map):
    layers, tokens, width = saved_inputs.shape
    rank = proj_in.shape[1]
    rows = weights.shape[1]
    n_dp, n_tensor, n_layer = (lax.axis_size(k) for k in ("dp", "tensor", "layer"))
    n_y = n_tensor // 2
    half = tokens // 2
    t, b = lax.axis_index("tensor"), lax.axis_index("layer")
    x, y = t & 1, t >> 1
    core = lax.axis_index("dp") & 1
    place = jnp.stack([x, core, b, y]).astype(jnp.int32)
    along_y = [[2 * k + j for k in range(n_y)] for j in range(2)]
    along_xz = [[2 * n_layer * k + j for j in range(2 * n_layer)] for k in range(n_y)]
    along_dp_x = [
        [d * n_tensor + 2 * k + j for d in range(n_dp) for j in range(2)] for k in range(n_y)
    ]
    across = [
        (d * n_tensor + k, (d ^ 2) * n_tensor + (k ^ 1)) for d in range(n_dp) for k in range(n_tensor)
    ]
    beside = [(k, k ^ 1) for k in range(n_tensor)]
    flat = pltpu.with_memory_space_constraint(
        weights.reshape(layers, rows, n_tensor, width), pltpu.HBM
    )
    owners = jnp.arange(n_layer, dtype=jnp.int32)
    layer_of = jnp.sum(
        owners[None, :] * (owner_map[None, :] == owners[:, None]).astype(jnp.int32), axis=1
    )

    gathered = exchange(
        jnp.broadcast_to(output_grad, (n_tensor, *output_grad.shape)), "tensor"
    )
    one = core.astype(jnp.int32).reshape(1)
    own, passed, near, far = ([None] * layers for _ in range(4))
    for level, pieces in ((2, 1), (3, 0), (1, 2), (0, 2)):
        own[level], passed[level] = features_first(flat, level, one, pieces)

    def over_both(values):
        return [
            in_hbm(lax.ppermute(values[0], ("dp", "tensor"), across)),
            in_hbm(lax.ppermute(values[1], "tensor", beside)),
        ]

    def to_other_core(values):
        return [in_hbm(lax.ppermute(v, "dp", [(d, d ^ 1) for d in range(n_dp)])) for v in values]

    near[2] = [in_hbm(lax.ppermute(passed[2][0], ("dp", "tensor"), across))]
    in_parts = in_factor_parts(saved_inputs, proj_in)
    gathered, own[3], own[2], own[1], passed[1], in_parts, place, layer_of = after(
        (gathered, own[3], own[2], own[1], passed[1], in_parts, place, layer_of)
    )

    partial = first_partial(gathered, own[3], in_parts)
    arrived = exchange(partial, ("tensor", "layer"), along_xz)
    total, copies, above_3, above_2 = settle_first(place, arrived, gathered)

    passed[1], proj_out, _ = after((passed[1], proj_out, total))
    other_proj = lax.ppermute(proj_out, "tensor", beside)
    pair_proj = jnp.where(
        x == 0, jnp.stack([proj_out, other_proj], 1), jnp.stack([other_proj, proj_out], 1)
    )
    shifted = [pair_proj[0]] + [
        lax.ppermute(pair_proj[0], "layer", [(z, z ^ k) for z in range(n_layer)])
        for k in range(1, n_layer)
    ]
    last_proj = jnp.stack(
        [
            sum_of(jnp.where((b ^ k) == z, shifted[k], 0) for k in range(n_layer))
            for z in range(n_layer)
        ]
    ).astype(BF16)
    near[1] = over_both(passed[1])
    near[2], _ = after((near[2], total))
    far[2] = to_other_core(near[2])
    gathered = exchange(copies, "tensor", along_y)
    gathered, own[0], passed[0], pair_proj, last_proj = after(
        (gathered, own[0], passed[0], pair_proj, last_proj)
    )
    partial = pair_partial(place, gathered, [own[2], *near[2], *far[2]])
    arrived = exchange(partial, "layer")
    total, copies, above_1, ins = settle(arrived, total)

    near[1], _ = after((near[1], total))
    far[1] = to_other_core(near[1])
    passed[0], _ = after((passed[0], near[1]))
    near[0] = over_both(passed[0])
    gathered = exchange(copies, "tensor", along_y)
    far[1], gathered = after((far[1], gathered))
    partial = pair_partial_scored(
        place,
        layer_of,
        gathered,
        [own[1], *near[1], *far[1]],
        [above_3, above_2, above_1],
        pair_proj,
        last_proj,
        ins,
    )
    partial, near[0] = after((partial, near[0]))
    far[0] = to_other_core(near[0])
    arrived = exchange(partial, "layer")
    arrived, far[0] = after((arrived, far[0]))
    total, copies = settle_scored(arrived, total)

    gathered = exchange(copies, "tensor", along_y)
    summed = gathered[:, 2 * width :].astype(F32).sum(axis=0).astype(BF16)
    every = exchange(
        jnp.broadcast_to(summed, (2 * n_dp, *summed.shape)), ("dp", "tensor"), along_dp_x
    )
    whole = every.reshape(n_dp, 2, rank // 4, 4, rank).astype(F32).sum(axis=1)
    whole = jnp.swapaxes(whole, 1, 2).reshape(n_dp, rank * rank).astype(BF16)
    scored = dot(whole, query_grads[0], NT)
    high = scored.astype(BF16)
    low = (scored - high.astype(F32)).astype(BF16)
    carried = jnp.concatenate([high, low], axis=1)[:, None, :]
    carried = jnp.broadcast_to(carried, (n_dp, 16, carried.shape[2]))
    partial = last_partial(
        place, gathered, [own[0], *near[0], *far[0]], total, carried.shape[1]
    )
    partial = put_under(partial, carried)
    arrived = exchange(partial, ("tensor", "layer"), along_xz)
    input_grad, scores = finish(place, arrived)
    return input_grad, scores


def solution(mesh):
    in_specs = (
        P(None, "dp", ("tensor", "layer")),
        P("dp", ("tensor", "layer")),
        P(None, "tensor", None, "layer", None),
        P(None, None, ("tensor", "layer")),
        P(None, None, ("tensor", "layer")),
        P("layer", ("dp", "tensor"), None),
        P(),
    )
    out_specs = (P("dp", ("tensor", "layer")), P("layer", ("dp", "tensor")))
    return jax.shard_map(
        on_device, mesh=mesh, in_specs=in_specs, out_specs=out_specs, check_vma=False
    )
```

```python
import jax
import jax.numpy as jnp
from jax import lax
from jax.experimental import pallas as pl
from jax.experimental.pallas import tpu as pltpu
from jax.sharding import PartitionSpec as P

NT = (((1,), (1,)), ((), ()))
NN = (((1,), (0,)), ((), ()))
F32 = jnp.float32
BF16 = jnp.bfloat16
WIDE = pl.BlockSpec(memory_space=pltpu.VMEM)
SCALARS = pl.BlockSpec(memory_space=pltpu.SMEM)
after = lax.optimization_barrier


def limit(mib):
    return pltpu.CompilerParams(vmem_limit_bytes=mib << 20)


def dot(left, right, dims=NN):
    return lax.dot_general(left, right, dims, preferred_element_type=F32)


def sum_of(terms):
    total = None
    for term in terms:
        total = term if total is None else total + term
    return total


def in_hbm(value):
    return pltpu.with_memory_space_constraint(value, pltpu.HBM)


def local_call(body, outs, operands, scalars=(), cost=None, to_hbm=()):
    def whole(out):
        return pl.BlockSpec(out[0], lambda: (0,) * len(out[0]))

    return pl.pallas_call(
        body,
        in_specs=[SCALARS] * len(scalars) + [WIDE] * len(operands),
        out_specs=[whole(out) if i in to_hbm else WIDE for i, out in enumerate(outs)],
        out_shape=[
            pltpu.HBM(*out) if i in to_hbm else jax.ShapeDtypeStruct(*out)
            for i, out in enumerate(outs)
        ],
        compiler_params=limit(8),
        cost_estimate=cost,
    )(*scalars, *operands)


def streamed_call(body, outs, weights, operands, scalars, scratch=(), late=()):
    rows, width = weights[0].shape[1:]
    tokens = operands[0].shape[-1]
    cells = sum(w.shape[0] for w in weights)
    groups = rows // width
    moved = [*weights, *late]
    sizes = [
        len(scalars), len(moved), len(operands), len(outs), len(moved), len(scratch),
    ]

    def kernel(*refs):
        parts, at = [], 0
        for size in sizes:
            parts.append(refs[at : at + size])
            at += size
        scalar_refs, far_refs, operand_refs, out_refs, held_refs, scratch_refs = parts
        sems = refs[-1]
        count = len(weights)

        def copies(n):
            if n < 0:
                return [
                    pltpu.make_async_copy(far_refs[k], held_refs[k], sems.at[k, 0])
                    for k in range(count, len(moved))
                ]
            rows_of = pl.ds(n * width, width)
            return [
                pltpu.make_async_copy(
                    far_refs[k].at[:, rows_of], held_refs[k].at[:, rows_of], sems.at[k, n]
                )
                for k in range(count)
            ]

        for n in [*range(groups), -1]:
            for copy in copies(n):
                copy.start()

        def fetch(n, which=slice(None)):
            for copy in copies(n)[which]:
                copy.wait()

        body(
            fetch,
            scalar_refs,
            held_refs[:count],
            [*operand_refs, *held_refs[count:]],
            out_refs,
            scratch_refs,
        )

    return pl.pallas_call(
        kernel,
        in_specs=[SCALARS] * len(scalars)
        + [pl.BlockSpec(memory_space=pltpu.HBM)] * len(moved)
        + [WIDE] * len(operands),
        out_specs=[WIDE] * len(outs),
        out_shape=[jax.ShapeDtypeStruct(*out) for out in outs],
        scratch_shapes=[pltpu.VMEM(w.shape, w.dtype) for w in moved]
        + list(scratch)
        + [pltpu.SemaphoreType.DMA((len(moved), groups))],
        compiler_params=limit(20),
        cost_estimate=pl.CostEstimate(
            flops=2 * cells * width * rows * tokens,
            bytes_accessed=2 * cells * width * rows,
            transcendentals=0,
        ),
    )(*scalars, *moved, *operands)


def features_first(weights, level, core, pieces):
    _, rows, cells, width = weights.shape
    step, half = 512, cells // 2
    deep = half // max(pieces, 1)

    def body(core_ref, w_ref, o_ref, *s_refs):
        o_ref[...] = jnp.swapaxes(w_ref[0], 0, 1)
        for i, s_ref in enumerate(s_refs):
            s_ref[...] = o_ref[pl.ds(half * core_ref[0] + deep * i, deep)]

    depths = [cells] + [deep] * pieces
    parts = pl.pallas_call(
        body,
        grid_spec=pltpu.PrefetchScalarGridSpec(
            num_scalar_prefetch=1,
            grid=(rows // step,),
            in_specs=[pl.BlockSpec((1, step, cells, width), lambda n, c: (level, n, 0, 0))],
            out_specs=[pl.BlockSpec((k, step, width), lambda n, c: (0, n, 0)) for k in depths],
        ),
        out_shape=[pltpu.HBM((k, rows, width), weights.dtype) for k in depths],
        compiler_params=limit(16),
        cost_estimate=pl.CostEstimate(
            flops=0, bytes_accessed=5 * rows * cells * width, transcendentals=0
        ),
    )(core, weights)
    return in_hbm(parts[0]), [in_hbm(part) for part in parts[1:]]


def in_factor_parts(saved_inputs, proj_in):
    layers, tokens, width = saved_inputs.shape
    rank = proj_in.shape[1]
    half = tokens // 2

    def body(x_ref, p_ref, o_ref):
        for h in range(2):
            part = dot(p_ref[0], x_ref[0, h * half : (h + 1) * half], NT)
            o_ref[h, 0] = part.astype(o_ref.dtype)

    return pl.pallas_call(
        body,
        grid=(layers,),
        in_specs=[
            pl.BlockSpec((1, tokens, width), lambda k: (k, 0, 0)),
            pl.BlockSpec((1, rank, width), lambda k: (k, 0, 0)),
        ],
        out_specs=pl.BlockSpec((2, 1, rank, half), lambda k: (0, k, 0, 0)),
        out_shape=jax.ShapeDtypeStruct((2, layers, rank, half), BF16),
        compiler_params=limit(8),
        cost_estimate=pl.CostEstimate(
            flops=2 * layers * tokens * width * rank,
            bytes_accessed=2 * layers * tokens * width,
            transcendentals=0,
        ),
    )(saved_inputs, proj_in).reshape(2 * layers, rank, half)


def first_partial(gathered, weight, extra):
    cells, tokens, width = gathered.shape
    groups = weight.shape[1] // width
    half = tokens // 2

    def body(fetch, _, weight_refs, operand_refs, out_refs, __):
        (w_ref,), (g_ref, e_ref), (o_ref,) = weight_refs, operand_refs, out_refs
        o_ref[:, width:] = e_ref[...]
        for n in range(groups):
            fetch(n)
            for h in range(2):
                total = sum_of(
                    dot(
                        w_ref[a, n * width : (n + 1) * width],
                        g_ref[a, h * half : (h + 1) * half],
                        NT,
                    )
                    for a in range(cells)
                )
                o_ref[h * groups + n, :width] = total.astype(o_ref.dtype)

    return streamed_call(
        body,
        [((2 * groups, width + extra.shape[1], half), BF16)],
        [weight],
        [gathered, extra],
        [],
    )[0]


def pair_totals(fetch, s_ref, g_ref, w_refs, n):
    own_ref, *others = w_refs
    cells, _, width = own_ref.shape
    half = cells // 2
    deep = others[0].shape[0]
    pieces = half // deep
    x, core = s_ref[0], s_ref[1]
    cut = slice(n * width, (n + 1) * width)
    fetch(n, slice(0, 1))
    yield x, sum_of(
        dot(own_ref[a, cut], g_ref[a // 2, (a % 2) * width : (a % 2 + 1) * width])
        for a in range(cells)
    )
    fetch(n, slice(1, None))
    yield 1 - x, sum_of(
        dot(
            refs[i // deep][i % deep, cut],
            g_ref[(half // 2) * first + i // 2, (i % 2) * width : (i % 2 + 1) * width],
        )
        for first, refs in ((core, others[:pieces]), (1 - core, others[pieces:]))
        for i in range(half)
    )


def pair_partial(place, gathered, held):
    width = held[0].shape[2]
    groups = held[0].shape[1] // width

    def body(fetch, scalar_refs, w_refs, operand_refs, out_refs, _):
        (s_ref,), (g_ref,), (o_ref,) = scalar_refs, operand_refs, out_refs
        whole = sum_of(g_ref[k, 2 * width :].astype(F32) for k in range(g_ref.shape[0]))
        for n in range(groups):
            o_ref[n, 2 * width :] = whole.astype(o_ref.dtype)
            for column, total in pair_totals(fetch, s_ref, g_ref, w_refs, n):
                start = pl.multiple_of(column * width, width)
                o_ref[n, pl.ds(start, width)] = total.astype(o_ref.dtype)

    return streamed_call(
        body, [((groups, *gathered.shape[1:]), BF16)], held, [gathered], [place]
    )[0]


def pair_partial_scored(place, layer_of, gathered, held, grads, proj, last_proj, ins):
    width = held[0].shape[2]
    groups = held[0].shape[1] // width
    layers, rank, tokens = ins.shape
    quarter = rank // 4

    def body(fetch, scalar_refs, w_refs, operand_refs, out_refs, scratch_refs):
        s_ref, l_ref = scalar_refs
        g_ref, *grad_refs, p_ref, q_ref, i_ref = operand_refs
        (o_ref,), (f_ref,) = out_refs, scratch_refs

        def factor(level, ref):
            return dot(p_ref[level, 0], ref[:width]) + dot(p_ref[level, 1], ref[width : 2 * width])

        for k, ref in enumerate(grad_refs):
            f_ref[layers - 1 - k] = factor(layers - 1 - k, ref).astype(f_ref.dtype)
        final = factor(0, grad_refs[-1])
        for n in range(groups):
            for column, total in pair_totals(fetch, s_ref, g_ref, w_refs, n):
                start = pl.multiple_of(column * width, width)
                rounded = total.astype(o_ref.dtype)
                o_ref[n, pl.ds(start, width)] = rounded
                final = final + dot(q_ref[n, column], rounded)
        f_ref[0] = final.astype(f_ref.dtype)
        for o in range(layers):
            block = dot(f_ref[l_ref[o]], i_ref[l_ref[o]], NT).astype(o_ref.dtype)
            o_ref[o, 2 * width :] = jnp.concatenate(
                [block[quarter * j : quarter * (j + 1)] for j in range(4)], axis=1
            )

    return streamed_call(
        body,
        [((groups, 2 * width + quarter, tokens), BF16)],
        held,
        [gathered, *grads, proj, last_proj, ins],
        [place, layer_of],
        [pltpu.VMEM((layers, rank, tokens), BF16)],
    )[0]


def last_partial(place, gathered, held, kept, under):
    width = held[0].shape[2]
    groups = held[0].shape[1] // width

    def body(fetch, scalar_refs, w_refs, operand_refs, out_refs, _):
        (s_ref,), (g_ref, t_ref), (o_ref,) = scalar_refs, operand_refs, out_refs
        for k in range(2 * groups):
            o_ref[k, width:] = jnp.zeros((under, o_ref.shape[2]), o_ref.dtype)
        fetch(-1)
        for n in range(groups):
            for column, total in pair_totals(fetch, s_ref, g_ref, w_refs, n):
                start = pl.multiple_of(column * width, width)
                mine = t_ref[pl.ds(start, width)]
                total = total + jnp.where(n == s_ref[2], mine, jnp.zeros_like(mine))
                o_ref[groups * column + n, :width] = total.astype(o_ref.dtype)

    return streamed_call(
        body,
        [((2 * groups, width + under, gathered.shape[2]), BF16)],
        held,
        [gathered],
        [place],
        late=[kept],
    )[0]


def put_under(partial, extra):
    blocks, deep, _ = partial.shape
    groups, rows, _ = extra.shape

    def body(_, e_ref, o_ref, sems):
        copies = [
            pltpu.make_async_copy(
                e_ref.at[k % groups], o_ref.at[k, pl.ds(deep - rows, rows)], sems.at[k]
            )
            for k in range(blocks)
        ]
        for copy in copies:
            copy.start()
        for copy in copies:
            copy.wait()

    return pl.pallas_call(
        body,
        in_specs=[pl.BlockSpec(memory_space=pl.ANY), WIDE],
        out_specs=pl.BlockSpec(memory_space=pl.ANY),
        out_shape=jax.ShapeDtypeStruct(partial.shape, partial.dtype),
        scratch_shapes=[pltpu.SemaphoreType.DMA((blocks,))],
        input_output_aliases={0: 0},
        compiler_params=limit(4),
    )(partial, extra)


def settle_first(place, arrived, gathered):
    blocks, deep, half = arrived.shape
    width = gathered.shape[2]
    groups = blocks // 2

    def body(s_ref, r_ref, g_ref, t_ref, c_ref, b_ref, m_ref):
        x, y = s_ref[0], s_ref[3]
        for k in range(2):
            rows_of = slice(k * width, (k + 1) * width)
            start = g_ref[2 * y + k, pl.ds(pl.multiple_of(x * half, half), half)].astype(F32).T
            b_ref[rows_of] = start.astype(BF16)
            total = start + sum_of(r_ref[groups * k + z, :width].astype(F32) for z in range(groups))
            t_ref[rows_of] = total
            rounded = total.astype(BF16)
            m_ref[rows_of] = rounded
            for j in range(c_ref.shape[0]):
                c_ref[j, rows_of] = rounded
        ins = sum_of(r_ref[k, width:].astype(F32) for k in range(blocks)).astype(BF16)
        for j in range(c_ref.shape[0]):
            c_ref[j, 2 * width :] = ins

    return local_call(
        body,
        [
            ((2 * width, half), F32),
            ((gathered.shape[0] // 2, 2 * width + deep - width, half), BF16),
            ((2 * width, half), BF16),
            ((2 * width, half), BF16),
        ],
        [arrived, gathered],
        [place],
        to_hbm=(0, 1, 2, 3),
    )


def settle(arrived, total):
    groups, deep, half = arrived.shape
    depth = total.shape[0]

    def body(r_ref, t_ref, o_ref, c_ref, m_ref, i_ref):
        value = t_ref[...] + sum_of(r_ref[z, :depth].astype(F32) for z in range(groups))
        o_ref[...] = value
        rounded = value.astype(BF16)
        m_ref[...] = rounded
        for j in range(c_ref.shape[0]):
            c_ref[j] = rounded
        i_ref[...] = r_ref[:, depth:]

    return local_call(
        body,
        [
            (total.shape, F32),
            ((groups, depth, half), BF16),
            (total.shape, BF16),
            ((groups, deep - depth, half), BF16),
        ],
        [arrived, total],
    )


def settle_scored(arrived, total):
    groups, deep, half = arrived.shape
    depth = total.shape[0]

    def body(r_ref, t_ref, o_ref, c_ref):
        value = t_ref[...] + sum_of(r_ref[z, :depth].astype(F32) for z in range(groups))
        o_ref[...] = value
        rounded = value.astype(BF16)
        blocks = sum_of(r_ref[z, depth:].astype(F32) for z in range(groups)).astype(BF16)
        for j in range(c_ref.shape[0]):
            c_ref[j, :depth] = rounded
            c_ref[j, depth:] = blocks

    return local_call(
        body,
        [(total.shape, F32), ((groups, deep, half), BF16)],
        [arrived, total],
        to_hbm=(0,),
    )


def finish(place, arrived):
    blocks, _, half = arrived.shape
    groups = blocks // 2
    width = half

    def body(s_ref, r_ref, o_ref, e_ref):
        for k in range(2):
            value = sum_of(r_ref[groups * k + z, :width].astype(F32) for z in range(groups))
            o_ref[k * half : (k + 1) * half] = value.T.astype(o_ref.dtype)
        ends = sum_of(r_ref[groups * s_ref[0] + z, width:].astype(F32) for z in range(groups))
        e_ref[...] = ends[:1, : half // 2] + ends[:1, half // 2 :]

    return local_call(
        body, [((2 * half, width), BF16), ((1, half // 2), F32)], [arrived], [place]
    )


def exchange(blocks, axes, groups=None):
    return lax.all_to_all(blocks, axes, 0, 0, tiled=True, axis_index_groups=groups)


def on_device(saved_inputs, output_grad, weights, proj_in, proj_out, query_grads, owner_map):
    layers, tokens, width = saved_inputs.shape
    rank = proj_in.shape[1]
    rows = weights.shape[1]
    n_dp, n_tensor, n_layer = (lax.axis_size(k) for k in ("dp", "tensor", "layer"))
    n_y = n_tensor // 2
    half = tokens // 2
    t, b = lax.axis_index("tensor"), lax.axis_index("layer")
    x, y = t & 1, t >> 1
    core = lax.axis_index("dp") & 1
    place = jnp.stack([x, core, b, y]).astype(jnp.int32)
    along_y = [[2 * k + j for k in range(n_y)] for j in range(2)]
    along_xz = [[2 * n_layer * k + j for j in range(2 * n_layer)] for k in range(n_y)]
    along_dp_x = [
        [d * n_tensor + 2 * k + j for d in range(n_dp) for j in range(2)] for k in range(n_y)
    ]
    across = [
        (d * n_tensor + k, (d ^ 2) * n_tensor + (k ^ 1)) for d in range(n_dp) for k in range(n_tensor)
    ]
    beside = [(k, k ^ 1) for k in range(n_tensor)]
    flat = pltpu.with_memory_space_constraint(
        weights.reshape(layers, rows, n_tensor, width), pltpu.HBM
    )
    owners = jnp.arange(n_layer, dtype=jnp.int32)
    layer_of = jnp.sum(
        owners[None, :] * (owner_map[None, :] == owners[:, None]).astype(jnp.int32), axis=1
    )

    gathered = exchange(
        jnp.broadcast_to(output_grad, (n_tensor, *output_grad.shape)), "tensor"
    )
    one = core.astype(jnp.int32).reshape(1)
    own, passed, near, far = ([None] * layers for _ in range(4))
    for level, pieces in ((2, 1), (3, 0), (1, 2), (0, 2)):
        own[level], passed[level] = features_first(flat, level, one, pieces)

    def over_both(values):
        return [
            in_hbm(lax.ppermute(values[0], ("dp", "tensor"), across)),
            in_hbm(lax.ppermute(values[1], "tensor", beside)),
        ]

    def to_other_core(values):
        return [in_hbm(lax.ppermute(v, "dp", [(d, d ^ 1) for d in range(n_dp)])) for v in values]

    near[2] = [in_hbm(lax.ppermute(passed[2][0], ("dp", "tensor"), across))]
    in_parts = in_factor_parts(saved_inputs, proj_in)
    gathered, own[3], own[2], own[1], passed[1], in_parts, place, layer_of = after(
        (gathered, own[3], own[2], own[1], passed[1], in_parts, place, layer_of)
    )

    partial = first_partial(gathered, own[3], in_parts)
    arrived = exchange(partial, ("tensor", "layer"), along_xz)
    total, copies, above_3, above_2 = settle_first(place, arrived, gathered)

    passed[1], proj_out, _ = after((passed[1], proj_out, total))
    other_proj = lax.ppermute(proj_out, "tensor", beside)
    pair_proj = jnp.where(
        x == 0, jnp.stack([proj_out, other_proj], 1), jnp.stack([other_proj, proj_out], 1)
    )
    shifted = [pair_proj[0]] + [
        lax.ppermute(pair_proj[0], "layer", [(z, z ^ k) for z in range(n_layer)])
        for k in range(1, n_layer)
    ]
    last_proj = jnp.stack(
        [
            sum_of(jnp.where((b ^ k) == z, shifted[k], 0) for k in range(n_layer))
            for z in range(n_layer)
        ]
    ).astype(BF16)
    near[1] = over_both(passed[1])
    near[2], _ = after((near[2], total))
    far[2] = to_other_core(near[2])
    gathered = exchange(copies, "tensor", along_y)
    gathered, own[0], passed[0], pair_proj, last_proj = after(
        (gathered, own[0], passed[0], pair_proj, last_proj)
    )
    partial = pair_partial(place, gathered, [own[2], *near[2], *far[2]])
    arrived = exchange(partial, "layer")
    total, copies, above_1, ins = settle(arrived, total)

    near[1], _ = after((near[1], total))
    far[1] = to_other_core(near[1])
    passed[0], _ = after((passed[0], near[1]))
    near[0] = over_both(passed[0])
    gathered = exchange(copies, "tensor", along_y)
    far[1], gathered = after((far[1], gathered))
    partial = pair_partial_scored(
        place,
        layer_of,
        gathered,
        [own[1], *near[1], *far[1]],
        [above_3, above_2, above_1],
        pair_proj,
        last_proj,
        ins,
    )
    partial, near[0] = after((partial, near[0]))
    far[0] = to_other_core(near[0])
    arrived = exchange(partial, "layer")
    arrived, far[0] = after((arrived, far[0]))
    total, copies = settle_scored(arrived, total)

    gathered = exchange(copies, "tensor", along_y)
    summed = gathered[:, 2 * width :].astype(F32).sum(axis=0).astype(BF16)
    every = exchange(
        jnp.broadcast_to(summed, (2 * n_dp, *summed.shape)), ("dp", "tensor"), along_dp_x
    )
    whole = every.reshape(n_dp, 2, rank // 4, 4, rank).astype(F32).sum(axis=1)
    whole = jnp.swapaxes(whole, 1, 2).reshape(n_dp, rank * rank).astype(BF16)
    scored = dot(whole, query_grads[0], NT)
    high = scored.astype(BF16)
    low = (scored - high.astype(F32)).astype(BF16)
    carried = jnp.concatenate([high, low], axis=1)[:, None, :]
    carried = jnp.broadcast_to(carried, (n_dp, 16, carried.shape[2]))
    partial = last_partial(
        place, gathered, [own[0], *near[0], *far[0]], total, carried.shape[1]
    )
    partial = put_under(partial, carried)
    arrived = exchange(partial, ("tensor", "layer"), along_xz)
    input_grad, scores = finish(place, arrived)
    return input_grad, scores


def solution(mesh):
    in_specs = (
        P(None, "dp", ("tensor", "layer")),
        P("dp", ("tensor", "layer")),
        P(None, "tensor", None, "layer", None),
        P(None, None, ("tensor", "layer")),
        P(None, None, ("tensor", "layer")),
        P("layer", ("dp", "tensor"), None),
        P(),
    )
    out_specs = (P("dp", ("tensor", "layer")), P("layer", ("dp", "tensor")))
    return jax.shard_map(
        on_device, mesh=mesh, in_specs=in_specs, out_specs=out_specs, check_vma=False
    )
```
